32 devices in a mesh: dp: 8 (over z, y), tensor: 4 (over x, core).
Axes of the slice: x: 2, y: 2, z: 4, core: 2. Of those that a mesh axis runs over, the one named last changes fastest.
Arguments:
- tokens: bfloat16 [8192, 1024], P(('dp', 'tensor')), may hold values from -6 to 6
- segment_ids: int32 [8, 1024], P('dp'), may hold values from 0 to 5, as said below
- positions: int32 [8, 1024], P('dp'), may hold values from 0 to 1023, as said below
- w_query: bfloat16 [1024, 2048], P('dp', 'tensor'), may hold values from -0.1875 to 0.1875
- key_projection: bfloat16 [1024, 1024], P('dp', 'tensor'), may hold values from -0.1875 to 0.1875
- value_projection: bfloat16 [1024, 1024], P('dp', 'tensor'), may hold values from -0.1875 to 0.1875
- w_out: bfloat16 [2048, 1024], P('tensor', 'dp'), may hold values from -0.5 to 0.5
- w_gate: bfloat16 [1024, 3072], P('dp', 'tensor'), may hold values from -0.1875 to 0.1875
- w_up: bfloat16 [1024, 3072], P('dp', 'tensor'), may hold values from -0.1875 to 0.1875
- w_down: bfloat16 [3072, 1024], P('tensor', 'dp'), may hold values from -0.109375 to 0.109375
- gain_attn: bfloat16 [1024], P('dp'), may hold values from 0.5 to 1.5
- gain_mlp: bfloat16 [1024], P('dp'), may hold values from 0.5 to 1.5
- gain_query: bfloat16 [128], P('dp'), may hold values from 0.5 to 1.5
- gain_key: bfloat16 [128], P('dp'), may hold values from 0.5 to 1.5
- cotangent: bfloat16 [8192, 1024], P(('dp', 'tensor')), may hold values from -6 to 6
Outputs:
- activations: bfloat16 [8192, 1024], P(('dp', 'tensor'))
- d_tokens: float32 [8192, 1024], P(('dp', 'tensor'))
- grad_query: float32 [1024, 2048], P('dp', 'tensor')
- grad_key: float32 [1024, 1024], P('dp', 'tensor')
- grad_value: float32 [1024, 1024], P('dp', 'tensor')
- grad_out: float32 [2048, 1024], P('tensor', 'dp')
- grad_gate: float32 [1024, 3072], P('dp', 'tensor')
- grad_up: float32 [1024, 3072], P('dp', 'tensor')
- grad_down: float32 [3072, 1024], P('tensor', 'dp')
- grad_gain_attn: float32 [1024], P('dp')
- grad_gain_mlp: float32 [1024], P('dp')
- grad_gain_query: float32 [128], P('dp')
- grad_gain_key: float32 [128], P('dp')
The draws below stay inside these ranges and needn't reach their ends.
Inputs may be any that keep to these rules, and one draw needn't show every extreme that they name: `segment_ids`: within each sequence the document number starts at 0 and rises by one at each new document; a document holds 200 to 2000 tokens (never more than 1024), except the last of a sequence, which may be cut short at the sequence's end. The largest number is reached in every draw. `positions`: the offset of each token from the first token of its document.
All inputs are finite; a program needn't handle non-finite values.
Results may differ from the reference program's by a relative error of at most 0.02.
Values may be sent and summed in bfloat16 or wider, within the bound.
No kernel may reach another device: no remote copies, remote signals or barrier semaphores. Data moves between devices by JAX's collectives and lax.ppermute only.
A program may use at most 128 MiB of HBM per device.

```python
import jax
import jax.numpy as jnp
from jax import lax

MODEL_WIDTH = 1024
QUERY_HEADS = 16
KEY_VALUE_HEADS = 8
HEAD_SIZE = 128
FF = 3072
DOC_MIN = 200
DOC_MAX = 2000
SEQS = 8
LEN = 1024
TOKENS = 8192


def document_layout(key):
    longest = min(DOC_MAX, LEN)
    doc_slots = LEN // DOC_MIN + 1
    lengths = jax.random.randint(jax.random.fold_in(key, 11), (SEQS, doc_slots), DOC_MIN, longest + 1)
    seq_rows = jnp.arange(SEQS)[:, None]
    slot_cols = jnp.arange(doc_slots)[None, :]
    opening = (seq_rows == 0) & (slot_cols == 0)
    lengths = jnp.where(opening, longest, lengths)
    lengths = jnp.where((seq_rows == 1) & (slot_cols >= 0), DOC_MIN, lengths).astype(jnp.int32)
    doc_ends = jnp.cumsum(lengths, axis=1).astype(jnp.int32)
    doc_starts = doc_ends - lengths
    position_ids = jnp.arange(LEN, dtype=jnp.int32)
    segment = jnp.sum((doc_ends[:, None, :] <= position_ids[None, :, None]).astype(jnp.int32), axis=2).astype(jnp.int32)
    doc_begin = jnp.take_along_axis(doc_starts, segment, axis=1)
    return (segment, (position_ids[None, :] - doc_begin).astype(jnp.int32))


def draw_segment_ids(key, part):
    return document_layout(key)[0]


def draw_positions(key, part):
    return document_layout(key)[1]


def with_spikes(values, key, source, target, parts, factor):
    def block_of(dim):
        return (jnp.arange(values.shape[dim]) // (values.shape[dim] // parts)).reshape((-1,) + (1,) * (values.ndim - 1 - dim))

    near = jax.random.permutation(key, parts)[block_of(target)]
    second = (block_of(target) + parts // 2) % parts
    return jnp.where((block_of(source) == near) | (block_of(source) == second), factor * values, values)


def shard_levels(rng, extent, cuts, low, top_value):
    loudness, own = 1.0, jax.random.fold_in(rng, 6)
    for position, parts in cuts:
        steps = jnp.exp(jax.random.uniform(jax.random.fold_in(own, position), (parts,), jnp.float32, low / len(cuts), top_value / len(cuts)))
        loudness = loudness * jnp.repeat(steps, extent[position] // parts).reshape([-1 if axis == position else 1 for axis in range(len(extent))])
    return loudness


def normal_values(own_key, dims, scale, reach, cuts=(), kind=jnp.bfloat16):
    gain = shard_levels(own_key, dims, cuts, -0.22, 0.18) if cuts else 1.0
    array = jax.random.normal(own_key, dims, jnp.float32) * scale * gain
    return jnp.minimum(jnp.maximum(array, -reach), reach).astype(kind)


def gaussian_with(own_key, extent, spread, limit, split, heavy, held_as=jnp.bfloat16):
    entries = spread * jax.random.normal(own_key, extent, jnp.float32)
    if split:
        entries = entries * shard_levels(own_key, extent, split, -0.22, 0.18)
    return jnp.clip(with_spikes(entries, jax.random.fold_in(own_key, 3), *heavy), -limit, limit).astype(held_as)


def setup_inputs(seed: int = 0) -> dict:
    key_of = jax.random.split(jax.random.key(seed), 16)
    return {
        "tokens": normal_values(key_of[0], (TOKENS, MODEL_WIDTH), 1.0, 6.0, ((0, 32),)),
        "segment_ids": draw_segment_ids(jax.random.fold_in(key_of[15], 71), 0),
        "positions": draw_positions(jax.random.fold_in(key_of[15], 71), 0),
        "w_query": normal_values(key_of[3], (MODEL_WIDTH, QUERY_HEADS * HEAD_SIZE), MODEL_WIDTH ** -0.5, 0.1875, ((0, 8), (1, 4))),
        "key_projection": normal_values(key_of[4], (MODEL_WIDTH, KEY_VALUE_HEADS * HEAD_SIZE), MODEL_WIDTH ** -0.5, 0.1875, ((0, 8), (1, 4))),
        "value_projection": normal_values(key_of[5], (MODEL_WIDTH, KEY_VALUE_HEADS * HEAD_SIZE), MODEL_WIDTH ** -0.5, 0.1875, ((0, 8), (1, 4))),
        "w_out": normal_values(key_of[6], (QUERY_HEADS * HEAD_SIZE, MODEL_WIDTH), (QUERY_HEADS * HEAD_SIZE // 16) ** -0.5, 0.5, ((0, 4), (1, 8))),
        "w_gate": normal_values(key_of[7], (MODEL_WIDTH, FF), MODEL_WIDTH ** -0.5, 0.1875, ((0, 8), (1, 4))),
        "w_up": normal_values(key_of[8], (MODEL_WIDTH, FF), MODEL_WIDTH ** -0.5, 0.1875, ((0, 8), (1, 4))),
        "w_down": normal_values(key_of[9], (FF, MODEL_WIDTH), FF ** -0.5, 0.109375, ((0, 4), (1, 8))),
        "gain_attn": jnp.clip(1.0 + 0.1 * jax.random.normal(key_of[10], (MODEL_WIDTH,), jnp.float32), 0.5, 1.5).astype(jnp.bfloat16),
        "gain_mlp": jnp.clip(1.0 + 0.1 * jax.random.normal(key_of[11], (MODEL_WIDTH,), jnp.float32), 0.5, 1.5).astype(jnp.bfloat16),
        "gain_query": jnp.clip(1.0 + 0.1 * jax.random.normal(key_of[12], (HEAD_SIZE,), jnp.float32), 0.5, 1.5).astype(jnp.bfloat16),
        "gain_key": jnp.clip(1.0 + 0.1 * jax.random.normal(key_of[13], (HEAD_SIZE,), jnp.float32), 0.5, 1.5).astype(jnp.bfloat16),
        "cotangent": gaussian_with(key_of[14], (TOKENS, MODEL_WIDTH), 1.0, 6.0, ((0, 32),), (0, 1, 32, 2.75)),
    }


@jax.custom_vjp
def low(v):
    return lax.optimization_barrier(v.astype(jnp.bfloat16)).astype(jnp.float32)

@jax.custom_vjp
def reduced_backward(v):
    return v

def low_keep(v):
    return (low(v), None)

def low_pass(kept, grad):
    return (grad,)

def back_keep(v):
    return (v, None)

def back_low(kept, grad):
    return (low(grad),)
low.defvjp(low_keep, low_pass)
reduced_backward.defvjp(back_keep, back_low)
epsilon = 1e-06
rope_base = 1000000.0
masked_score = -1e+30
precise = lax.Precision.HIGHEST

def matrix_product(left, right):
    return jnp.dot(left, right, precision=precise, preferred_element_type=jnp.float32)

def rms_scale(values, row_gain):
    return values * lax.rsqrt(lax.optimization_barrier(jnp.mean(values * values, axis=-1, keepdims=True)) + epsilon) * row_gain

def rotate(values, cosine, sine):
    middle = values.shape[-1] // 2
    front_half = values[..., :middle]
    back_half = values[..., middle:]
    return jnp.concatenate([front_half * cosine - back_half * sine, back_half * cosine + front_half * sine], axis=-1)

def rope_tables(offsets, width):
    frequency = rope_base ** (-(2.0 * jnp.arange(width // 2, dtype=jnp.float32)) / width)
    angles = offsets.astype(jnp.float32)[:, None] * frequency[None, :]
    return (jnp.cos(angles)[:, None, :], jnp.sin(angles)[:, None, :])

def attend(queries, keys_rep, values_rep, segments):
    document_length = queries.shape[0]
    block = min(512, document_length)
    blocks = document_length // block
    q_blocks = queries.reshape(blocks, block, QUERY_HEADS, HEAD_SIZE)
    seg_blocks = segments.reshape(blocks, block)
    row_blocks = jnp.arange(document_length, dtype=jnp.int32).reshape(blocks, block)
    col_ids = jnp.arange(document_length, dtype=jnp.int32)
    score_scale = HEAD_SIZE ** (-0.5)

    @jax.checkpoint
    def one_block(items):
        q_block, seg_block, row_ids = items
        scores = jnp.einsum('qhd,khd->hqk', q_block, keys_rep, precision=precise) * score_scale
        scores = reduced_backward(scores)
        allowed = (seg_block[:, None] == segments[None, :]) & (col_ids[None, :] <= row_ids[:, None])
        scores = jnp.where(allowed[None], scores, masked_score)
        row_peak = lax.optimization_barrier(jnp.max(scores, axis=-1, keepdims=True))
        expd = jnp.exp(scores - row_peak)
        weights = low(expd / lax.optimization_barrier(jnp.sum(expd, axis=-1, keepdims=True)))
        return jnp.einsum('hqk,khd->qhd', weights, values_rep, precision=precise)
    attended = lax.map(one_block, (q_blocks, seg_blocks, row_blocks))
    return attended.reshape(document_length, QUERY_HEADS * HEAD_SIZE)

def sequence(x_seq, segments, offsets, params):
    w_query, key_projection, value_projection, w_out, w_gate, w_up, w_down, gain_attn, gain_mlp, gain_query, gain_key = params
    document_length = x_seq.shape[0]
    normalized_rows = low(rms_scale(x_seq, gain_attn))
    q_raw = reduced_backward(matrix_product(normalized_rows, w_query)).reshape(document_length, QUERY_HEADS, HEAD_SIZE)
    key_unrotated = reduced_backward(matrix_product(normalized_rows, key_projection)).reshape(document_length, KEY_VALUE_HEADS, HEAD_SIZE)
    value_projected = reduced_backward(matrix_product(normalized_rows, value_projection)).reshape(document_length, KEY_VALUE_HEADS, HEAD_SIZE)
    cosine, sine = rope_tables(offsets, HEAD_SIZE)
    queries = low(rotate(rms_scale(q_raw, gain_query), cosine, sine))
    keys = low(rotate(rms_scale(key_unrotated, gain_key), cosine, sine))
    values = low(value_projected)
    query_group = QUERY_HEADS // KEY_VALUE_HEADS
    attended = attend(queries, jnp.repeat(keys, query_group, axis=1), jnp.repeat(values, query_group, axis=1), segments)
    mixed = low(reduced_backward(attended))
    hidden = x_seq + reduced_backward(matrix_product(mixed, w_out))
    normed_mlp = low(rms_scale(hidden, gain_mlp))
    gate = reduced_backward(matrix_product(normed_mlp, w_gate))
    up_proj = reduced_backward(matrix_product(normed_mlp, w_up))
    act = low(jax.nn.silu(gate) * up_proj)
    return hidden + reduced_backward(matrix_product(act, w_down))

def reference(tokens, segment_ids, positions, w_query, key_projection, value_projection, w_out, w_gate, w_up, w_down, gain_attn, gain_mlp, gain_query, gain_key, cotangent):
    params = (w_query.astype(jnp.float32), key_projection.astype(jnp.float32), value_projection.astype(jnp.float32), w_out.astype(jnp.float32), w_gate.astype(jnp.float32), w_up.astype(jnp.float32), w_down.astype(jnp.float32), gain_attn.astype(jnp.float32), gain_mlp.astype(jnp.float32), gain_query.astype(jnp.float32), gain_key.astype(jnp.float32))
    inputs = tokens.astype(jnp.float32).reshape(SEQS, LEN, MODEL_WIDTH)

    def forward(x_all, weights):

        def per_sequence(items):
            return sequence(items[0], items[1], items[2], weights)
        return lax.map(per_sequence, (x_all, segment_ids, positions))
    result, pullback = jax.vjp(forward, inputs, params)
    d_inputs, d_params = pullback(cotangent.astype(jnp.float32).reshape(SEQS, LEN, MODEL_WIDTH))
    return (result.reshape(TOKENS, MODEL_WIDTH).astype(jnp.bfloat16), d_inputs.reshape(TOKENS, MODEL_WIDTH), d_params[0], d_params[1], d_params[2], d_params[3], d_params[4], d_params[5], d_params[6], d_params[7], d_params[8], d_params[9], d_params[10])
```

```python
import functools

import jax
import jax.numpy as jnp
from jax import lax
from jax.experimental import pallas as pl
from jax.experimental.pallas import tpu as pltpu
from jax.sharding import PartitionSpec as P

HEAD = 128
EPS = 1e-06
ROPE_BASE = 1000000.0
SCALE = HEAD ** (-0.5)
EXP2_SCALE = SCALE * 1.4426950408889634
F32 = jnp.float32
BF16 = jnp.bfloat16
VMEM_LIMIT = 60 * 1024 * 1024


def mm(a, b, ca=1, cb=0):
    return lax.dot_general(a, b, (((ca,), (cb,)), ((), ())), preferred_element_type=F32)


def call(kernel, grid, in_specs, out_specs, out_shape, flops, nbytes, scratch=()):
    return pl.pallas_call(
        kernel,
        out_shape=out_shape,
        grid_spec=pltpu.PrefetchScalarGridSpec(
            num_scalar_prefetch=1,
            grid=grid,
            in_specs=in_specs,
            out_specs=out_specs,
            scratch_shapes=list(scratch),
        ),
        compiler_params=pltpu.CompilerParams(
            dimension_semantics=("arbitrary",) * len(grid), vmem_limit_bytes=VMEM_LIMIT
        ),
        cost_estimate=pl.CostEstimate(flops=flops, bytes_accessed=nbytes, transcendentals=0),
    )


def whole(shape):
    return pl.BlockSpec(shape, lambda i, t: (0,) * len(shape))


def rows_at(rows, cols):
    return pl.BlockSpec((rows, cols), lambda i, t: (i, 0))


def rows_xor(rows, cols):
    return pl.BlockSpec((rows, cols), lambda i, t: (lax.bitwise_xor(i, t[0]), 0))


def qkv_kernel(kv_heads, group, t, x, gain, w, cos, sin, gq, gk, normed, packed, raw):
    u = x[...].astype(F32)
    r = lax.rsqrt(jnp.mean(u * u, axis=1, keepdims=True) + EPS)
    low = (u * r * gain[...]).astype(BF16)
    normed[...] = low
    y = mm(low, w[...])
    c = cos[...]
    s = sin[...]
    for h in range(kv_heads):
        base = h * (group + 2) * HEAD
        kept = h * (group + 1) * HEAD
        for j in range(group + 1):
            v = y[:, base + j * HEAD : base + (j + 1) * HEAD]
            raw[:, kept + j * HEAD : kept + (j + 1) * HEAD] = v
            scale = gq[...] if j < group else gk[...]
            v = v * lax.rsqrt(jnp.mean(v * v, axis=1, keepdims=True) + EPS) * scale
            v = v * c + pltpu.roll(v, HEAD // 2, 1) * s
            packed[:, base + j * HEAD : base + (j + 1) * HEAD] = v.astype(BF16)
        end = base + (group + 1) * HEAD
        packed[:, end : end + HEAD] = y[:, end : end + HEAD].astype(BF16)


def qkv_call(t, x, gain, w, cos, sin, gq, gk, rows, kv_heads, group):
    n, width = x.shape
    cols = w.shape[1]
    kept = kv_heads * (group + 1) * HEAD
    return call(
        functools.partial(qkv_kernel, kv_heads, group),
        (n // rows,),
        [
            rows_at(rows, width),
            whole(gain.shape),
            whole(w.shape),
            rows_xor(rows, HEAD),
            rows_xor(rows, HEAD),
            whole(gq.shape),
            whole(gk.shape),
        ],
        [rows_at(rows, width), rows_xor(rows, cols), rows_xor(rows, kept)],
        [
            jax.ShapeDtypeStruct((n, width), BF16),
            jax.ShapeDtypeStruct((n, cols), BF16),
            jax.ShapeDtypeStruct((n, kept), F32),
        ],
        2 * n * width * cols,
        n * width * 4 + width * cols * 2 + n * cols * 5,
    )(t, x, gain, w, cos, sin, gq, gk)


def weights_of(q, k, same, causal):
    e = jnp.exp2(mm(k, q, 1, 1) * EXP2_SCALE)
    keep = same if causal is None else same & causal
    return jnp.where(keep, e, 0.0)


def attn_forward_kernel(rows, blocks, group, t, packed, seg_col, seg_row, mixed, inv):
    causal = lax.broadcasted_iota(jnp.int32, (rows, rows), 0) <= lax.broadcasted_iota(
        jnp.int32, (rows, rows), 1
    )
    kc = group * HEAD
    for i in range(blocks):
        lo = i * rows
        at = pl.multiple_of(lax.bitwise_xor(i, t[0]) * rows, rows)
        sq = seg_row[:, lo : lo + rows]
        for j in range(group):
            q = packed[lo : lo + rows, j * HEAD : (j + 1) * HEAD]
            parts = []
            total = jnp.zeros((1, rows), F32)
            for b in range(i + 1):
                k = packed[b * rows : (b + 1) * rows, kc : kc + HEAD]
                same = seg_col[b * rows : (b + 1) * rows, :] == sq
                e = weights_of(q, k, same, causal if b == i else None)
                total = total + jnp.sum(e, axis=0, keepdims=True)
                parts.append(e)
            rec = 1.0 / total
            inv[0, j : j + 1, lo : lo + rows] = rec
            out = jnp.zeros((rows, HEAD), F32)
            for b in range(i + 1):
                v = packed[b * rows : (b + 1) * rows, kc + HEAD : kc + 2 * HEAD]
                out = out + mm((parts[b] * rec).astype(BF16), v, 0, 0)
            mixed[pl.ds(at, rows), j * HEAD : (j + 1) * HEAD] = out.astype(BF16)


def attn_forward(t, packed, seg_col, seg_row, rows, kv_heads, group):
    n = packed.shape[0]
    return call(
        functools.partial(attn_forward_kernel, rows, n // rows, group),
        (kv_heads,),
        [
            pl.BlockSpec((n, (group + 2) * HEAD), lambda h, t: (0, h)),
            whole(seg_col.shape),
            whole(seg_row.shape),
        ],
        [
            pl.BlockSpec((n, group * HEAD), lambda h, t: (0, h)),
            pl.BlockSpec((1, 8, n), lambda h, t: (h, 0, 0)),
        ],
        [
            jax.ShapeDtypeStruct((n, kv_heads * group * HEAD), BF16),
            jax.ShapeDtypeStruct((kv_heads, 8, n), F32),
        ],
        kv_heads * group * n * n * HEAD * 4,
        n * kv_heads * (group + 1) * HEAD * 4,
    )(t, packed, seg_col, seg_row)


def head_back(e, u, cos, sin, gain):
    e = e * cos - pltpu.roll(e, HEAD // 2, 1) * sin
    r = lax.rsqrt(jnp.mean(u * u, axis=1, keepdims=True) + EPS)
    ur = u * r
    dgain = jnp.sum(e * ur, axis=0, keepdims=True)
    ec = e * gain
    du = r * (ec - ur * jnp.mean(ur * ec, axis=1, keepdims=True))
    return du, dgain


def attn_backward_kernel(
    rows, blocks, group, t, packed, seg_col, seg_row, inv, dmix, raw, cos, sin, gq, gk, dpacked, dgain, dk, dv
):
    causal = lax.broadcasted_iota(jnp.int32, (rows, rows), 0) <= lax.broadcasted_iota(
        jnp.int32, (rows, rows), 1
    )
    kc = group * HEAD
    dk[...] = jnp.zeros_like(dk)
    dv[...] = jnp.zeros_like(dv)
    dgain[...] = jnp.zeros_like(dgain)
    for i in range(blocks):
        lo = i * rows
        at = pl.multiple_of(lax.bitwise_xor(i, t[0]) * rows, rows)
        sq = seg_row[:, lo : lo + rows]
        for j in range(group):
            q = packed[lo : lo + rows, j * HEAD : (j + 1) * HEAD]
            do = dmix[pl.ds(at, rows), j * HEAD : (j + 1) * HEAD]
            rec = inv[0, j : j + 1, lo : lo + rows]
            probs = []
            dprobs = []
            delta = jnp.zeros((1, rows), F32)
            for b in range(i + 1):
                here = slice(b * rows, (b + 1) * rows)
                k = packed[here, kc : kc + HEAD]
                v = packed[here, kc + HEAD : kc + 2 * HEAD]
                same = seg_col[here, :] == sq
                p = weights_of(q, k, same, causal if b == i else None) * rec
                dp = mm(v, do, 1, 1)
                delta = delta + jnp.sum(p * dp, axis=0, keepdims=True)
                dv[here, :] += mm(p.astype(BF16), do)
                probs.append(p)
                dprobs.append(dp)
            dq = jnp.zeros((rows, HEAD), F32)
            for b in range(i + 1):
                here = slice(b * rows, (b + 1) * rows)
                k = packed[here, kc : kc + HEAD]
                ds = (probs[b] * (dprobs[b] - delta)).astype(BF16)
                dk[here, :] += mm(ds, q)
                dq = dq + mm(ds, k, 0, 0)
            du, dg = head_back(
                dq * SCALE,
                raw[lo : lo + rows, j * HEAD : (j + 1) * HEAD],
                cos[lo : lo + rows, :],
                sin[lo : lo + rows, :],
                gq[...],
            )
            dgain[0, 0:1, :] += dg
            dpacked[pl.ds(at, rows), j * HEAD : (j + 1) * HEAD] = du.astype(BF16)
    for i in range(blocks):
        here = slice(i * rows, (i + 1) * rows)
        at = pl.multiple_of(lax.bitwise_xor(i, t[0]) * rows, rows)
        du, dg = head_back(
            dk[here, :] * SCALE, raw[here, kc : kc + HEAD], cos[here, :], sin[here, :], gk[...]
        )
        dgain[0, 1:2, :] += dg
        dpacked[pl.ds(at, rows), kc : kc + HEAD] = du.astype(BF16)
        dpacked[pl.ds(at, rows), kc + HEAD : kc + 2 * HEAD] = dv[here, :].astype(BF16)


def attn_backward(t, packed, seg_col, seg_row, inv, dmix, raw, cos, sin, gq, gk, rows, kv_heads, group):
    n = packed.shape[0]
    by_head = lambda width: pl.BlockSpec((n, width), lambda h, t: (0, h))
    return call(
        functools.partial(attn_backward_kernel, rows, n // rows, group),
        (kv_heads,),
        [
            by_head((group + 2) * HEAD),
            whole(seg_col.shape),
            whole(seg_row.shape),
            pl.BlockSpec((1, 8, n), lambda h, t: (h, 0, 0)),
            by_head(group * HEAD),
            by_head((group + 1) * HEAD),
            whole(cos.shape),
            whole(sin.shape),
            whole(gq.shape),
            whole(gk.shape),
        ],
        [by_head((group + 2) * HEAD), pl.BlockSpec((1, 8, HEAD), lambda h, t: (h, 0, 0))],
        [
            jax.ShapeDtypeStruct(packed.shape, BF16),
            jax.ShapeDtypeStruct((kv_heads, 8, HEAD), F32),
        ],
        kv_heads * group * n * n * HEAD * 10,
        n * kv_heads * (group + 1) * HEAD * 14,
        [pltpu.VMEM((n, HEAD), F32), pltpu.VMEM((n, HEAD), F32)],
    )(t, packed, seg_col, seg_row, inv, dmix, raw, cos, sin, gq, gk)


def mlp_kernel(ff, t, x, g, w, wd, act, dgu, dx, out):
    y = mm(x[...], w[...])
    gate = y[:, :ff]
    up = y[:, ff:]
    sig = 1.0 / (1.0 + jnp.exp(-gate))
    silu = gate * sig
    a = (silu * up).astype(BF16)
    act[...] = a
    da = mm(g[...], wd[...])
    dgu[:, :ff] = (da * up * sig * (1.0 + gate * (1.0 - sig))).astype(BF16)
    dgu[:, ff:] = (da * silu).astype(BF16)
    dx[...] = mm(dgu[...], w[...], 1, 1).astype(BF16)
    out[...] = mm(a, wd[...], 1, 1).astype(BF16)


def mlp_call(t, x, g, w, wd, rows):
    n, width = x.shape
    ff = wd.shape[1]
    return call(
        functools.partial(mlp_kernel, ff),
        (n // rows,),
        [rows_at(rows, width), rows_at(rows, width), whole(w.shape), whole(wd.shape)],
        [rows_at(rows, ff), rows_at(rows, 2 * ff), rows_at(rows, width), rows_at(rows, width)],
        [
            jax.ShapeDtypeStruct((n, ff), BF16),
            jax.ShapeDtypeStruct((n, 2 * ff), BF16),
            jax.ShapeDtypeStruct((n, width), BF16),
            jax.ShapeDtypeStruct((n, width), BF16),
        ],
        2 * n * width * ff * 6,
        n * width * 8 + width * ff * 6 + n * ff * 6,
    )(t, x, g, w, wd)


def xor_pairs(size, bits):
    return [(i, i ^ bits) for i in range(size)]


class Links:
    def __init__(self, dp, tensor):
        self.dp, self.tensor = dp, tensor
        self.direct = (dp, tensor) == (8, 4)
        self.d = lax.axis_index("dp")
        self.t = lax.axis_index("tensor")

    def over_dp(self, x, bits):
        return lax.ppermute(x, "dp", xor_pairs(self.dp, bits))

    def over_tensor(self, x, bits):
        return lax.ppermute(x, "tensor", xor_pairs(self.tensor, bits))

    def row_offset(self):
        return (self.t if self.direct else jnp.int32(0)).reshape(1)

    def columns_in(self, x):
        if not self.direct:
            return x
        n = x.shape[1] // 8
        order = [2 * p if p < 4 else 2 * (p - 4) + 1 for p in range(8)]
        return jnp.concatenate(
            [lax.dynamic_slice_in_dim(x, lax.bitwise_xor(self.d, k) * n, n, 1) for k in order], axis=1
        )

    def columns_out(self, x):
        if not self.direct:
            return x
        n = x.shape[1] // 8
        blocks = []
        for b in range(8):
            k = lax.bitwise_xor(self.d, b)
            blocks.append(lax.dynamic_slice_in_dim(x, ((k >> 1) + 4 * (k & 1)) * n, n, 1))
        return jnp.concatenate(blocks, axis=1)

    def gather_dp(self, x):
        if not self.direct:
            return lax.all_gather(x, "dp", axis=0, tiled=True)
        own = [x] + [self.over_dp(x, 2 * z) for z in (1, 2, 3)]
        return jnp.concatenate(own + [self.over_dp(b, 1) for b in own], axis=0)

    def scatter_dp(self, left, right):
        if not self.direct:
            return lax.psum_scatter(
                mm(left, right, 0, 0).astype(BF16), "dp", scatter_dimension=0, tiled=True
            ).astype(F32)
        half = left.shape[1] // 2
        quarter = half // 4
        got = self.over_dp(mm(left[:, half:], right, 0, 0).astype(BF16), 1)
        keep = lax.optimization_barrier(mm(left[:, :half], right, 0, 0).astype(BF16))
        total = None
        parts = []
        for z in range(4):
            here = slice(z * quarter, (z + 1) * quarter)
            s = keep[here].astype(F32) + got[here].astype(F32)
            parts.append(s if z == 0 else self.over_dp(s.astype(BF16), 2 * z).astype(F32))
        return parts[0] + parts[1] + parts[2] + parts[3]

    def gather_tensor(self, x):
        if not self.direct:
            return lax.all_gather(x, "tensor", axis=0, tiled=True)
        far = self.over_tensor(x, 2)
        return jnp.concatenate([x, self.over_tensor(x, 1), far, self.over_tensor(far, 1)], axis=0)

    def scatter_tensor(self, x):
        if not self.direct:
            return lax.psum_scatter(x, "tensor", scatter_dimension=0, tiled=True).astype(F32)
        n = x.shape[0] // 4
        block = lambda k: x[k * n : (k + 1) * n]
        far = block(2).astype(F32) + self.over_tensor(block(3), 1).astype(F32)
        near = block(0).astype(F32) + self.over_tensor(block(1), 1).astype(F32)
        return near + self.over_tensor(far.astype(BF16), 2).astype(F32)

    def total(self, x):
        if not self.direct:
            return lax.psum(x, ("dp", "tensor"))
        x = x + self.over_tensor(x, 1)
        x = x + self.over_tensor(x, 2)
        x = x + self.over_dp(x, 1)
        return x + self.over_dp(x, 2) + self.over_dp(x, 4) + self.over_dp(x, 6)

    def gather_gains(self, *gains):
        if not self.direct:
            return [lax.all_gather(g, "dp", axis=0, tiled=True) for g in gains]
        sizes = [g.shape[0] for g in gains]
        flat = jnp.concatenate(gains)[None, :]
        own = [flat] + [self.over_dp(flat, 2 * z) for z in (1, 2, 3)]
        near = jnp.concatenate(own, axis=0)
        table = jnp.concatenate([near, self.over_dp(near, 1)], axis=0)
        out, at = [], 0
        for index, size in enumerate(sizes):
            part = table[:, at : at + size]
            if index >= 2:
                rows = []
                for b in range(8):
                    k = lax.bitwise_xor(self.d, b)
                    rows.append(lax.dynamic_slice_in_dim(part, (k >> 1) + 4 * (k & 1), 1, 0))
                part = jnp.concatenate(rows, axis=0)
            out.append(part.reshape(-1))
            at += size
        return out


def norm_back(e, u, gain):
    r = lax.rsqrt(jnp.mean(u * u, axis=1, keepdims=True) + EPS)
    ur = u * r
    ec = e * gain
    return r * (ec - ur * jnp.mean(ur * ec, axis=1, keepdims=True)), jnp.sum(e * ur, axis=0)


def rope_tables(offsets):
    frequency = ROPE_BASE ** (-(2.0 * jnp.arange(HEAD // 2, dtype=F32)) / HEAD)
    angles = offsets.astype(F32)[:, None] * frequency[None, :]
    cos, sin = jnp.cos(angles), jnp.sin(angles)
    return jnp.concatenate([cos, cos], axis=1), jnp.concatenate([-sin, sin], axis=1)


def pack_heads(wq, wk, wv, group):
    parts = []
    for h in range(wk.shape[1] // HEAD):
        parts += [
            wq[:, h * group * HEAD : (h + 1) * group * HEAD],
            wk[:, h * HEAD : (h + 1) * HEAD],
            wv[:, h * HEAD : (h + 1) * HEAD],
        ]
    return jnp.concatenate(parts, axis=1)


def unpack_heads(w, kv_heads, group):
    q, k, v = [], [], []
    for h in range(kv_heads):
        base = h * (group + 2) * HEAD
        mid = base + group * HEAD
        q.append(w[:, base:mid])
        k.append(w[:, mid : mid + HEAD])
        v.append(w[:, mid + HEAD : mid + 2 * HEAD])
    join = lambda parts: jnp.concatenate(parts, axis=1)
    return join(q), join(k), join(v)


def body(
    dp,
    tensor,
    tokens,
    segment_ids,
    positions,
    w_query,
    key_projection,
    value_projection,
    w_out,
    w_gate,
    w_up,
    w_down,
    gain_attn,
    gain_mlp,
    gain_query,
    gain_key,
    cotangent,
):
    links = Links(dp, tensor)
    rows = tokens.shape[0]
    kv_heads = key_projection.shape[1] // HEAD
    group = w_query.shape[1] // key_projection.shape[1]
    t = links.row_offset()

    w_qkv = links.gather_dp(pack_heads(w_query, key_projection, value_projection, group))
    w_o = links.gather_dp(w_out.T)
    w_gu = links.gather_dp(jnp.concatenate([w_gate, w_up], axis=1))
    w_d = links.gather_dp(w_down.T)
    g_attn, g_mlp, g_q, g_k = [
        g.astype(F32)[None, :] for g in links.gather_gains(gain_attn, gain_mlp, gain_query, gain_key)
    ]

    x_low = links.columns_in(tokens)
    cot_low = links.columns_in(cotangent)
    x_rows = links.gather_tensor(x_low)
    cot_rows = links.gather_tensor(cot_low)
    cos, sin = rope_tables(positions[0])
    seg_row = segment_ids
    seg_col = segment_ids.reshape(-1, 1)

    normed, packed, raw = qkv_call(
        t, x_rows, g_attn, w_qkv, cos, sin, g_q, g_k, rows, kv_heads, group
    )
    mixed, inv = attn_forward(t, packed, seg_col, seg_row, rows, kv_heads, group)
    branch = links.scatter_tensor(mm(mixed, w_o, 1, 1).astype(BF16))
    x = x_low.astype(F32)
    hidden = x + branch
    r = lax.rsqrt(jnp.mean(hidden * hidden, axis=1, keepdims=True) + EPS)
    normed_mlp = links.gather_tensor((hidden * r * g_mlp).astype(BF16))
    act, d_gu, d_norm, mlp_out = mlp_call(t, normed_mlp, cot_rows, w_gu, w_d, rows)
    d_norm_mlp = links.scatter_tensor(d_norm)
    d_part, d_gain_mlp = norm_back(d_norm_mlp, hidden, g_mlp)
    d_hidden = cot_low.astype(F32) + d_part
    branch_rows = links.gather_tensor(d_hidden.astype(BF16))
    activations = (hidden + links.scatter_tensor(mlp_out)).astype(BF16)

    grad_down = links.scatter_dp(cot_rows, act)
    grad_gu = links.scatter_dp(normed_mlp, d_gu)
    d_mixed = mm(branch_rows, w_o).astype(BF16)
    grad_out = links.scatter_dp(branch_rows, mixed)
    d_packed, d_gain_heads = attn_backward(
        t, packed, seg_col, seg_row, inv, d_mixed, raw, cos, sin, g_q, g_k, rows, kv_heads, group
    )
    grad_qkv = links.scatter_dp(normed, d_packed)
    d_norm_attn = links.scatter_tensor(mm(d_packed, w_qkv, 1, 1).astype(BF16))
    d_part, d_gain_attn = norm_back(d_norm_attn, x, g_attn)
    d_tokens = d_hidden + d_part

    head_gains = jnp.sum(d_gain_heads, axis=0)
    sums = links.total(
        jnp.concatenate(
            [
                links.columns_out(d_gain_attn[None, :]).reshape(-1, HEAD),
                links.columns_out(d_gain_mlp[None, :]).reshape(-1, HEAD),
                head_gains[:2],
            ],
            axis=0,
        )
    )
    width = tokens.shape[1]
    model_rows = width // HEAD
    n = width // dp
    m = HEAD // dp
    sum_attn = sums[:model_rows].reshape(-1)
    sum_mlp = sums[model_rows : 2 * model_rows].reshape(-1)
    shard = lambda v, size: lax.dynamic_slice_in_dim(v, links.d * size, size, 0)
    grad_query, grad_key, grad_value = unpack_heads(grad_qkv, kv_heads, group)
    ff = w_gate.shape[1]
    return (
        links.columns_out(activations),
        links.columns_out(d_tokens),
        grad_query,
        grad_key,
        grad_value,
        grad_out.T,
        grad_gu[:, :ff],
        grad_gu[:, ff:],
        grad_down.T,
        shard(sum_attn, n),
        shard(sum_mlp, n),
        shard(sums[2 * model_rows], m),
        shard(sums[2 * model_rows + 1], m),
    )


def solution(mesh):
    tokens = P(("dp", "tensor"), None)
    by_rows = P("dp", "tensor")
    by_columns = P("tensor", "dp")
    sequence = P("dp", None)
    gain = P("dp")
    return jax.shard_map(
        functools.partial(body, mesh.shape["dp"], mesh.shape["tensor"]),
        mesh=mesh,
        in_specs=(
            tokens,
            sequence,
            sequence,
            by_rows,
            by_rows,
            by_rows,
            by_columns,
            by_rows,
            by_rows,
            by_columns,
            gain,
            gain,
            gain,
            gain,
            tokens,
        ),
        out_specs=(
            tokens,
            tokens,
            by_rows,
            by_rows,
            by_rows,
            by_columns,
            by_rows,
            by_rows,
            by_columns,
            gain,
            gain,
            gain,
            gain,
        ),
        check_vma=False,
    )
```

```python
import functools

import jax
import jax.numpy as jnp
from jax import lax
from jax.experimental import pallas as pl
from jax.experimental.pallas import tpu as pltpu
from jax.sharding import PartitionSpec as P

HEAD = 128
EPS = 1e-06
ROPE_BASE = 1000000.0
SCALE = HEAD ** (-0.5)
EXP2_SCALE = SCALE * 1.4426950408889634
F32 = jnp.float32
BF16 = jnp.bfloat16
VMEM_LIMIT = 60 * 1024 * 1024
ORDER = (0, 2, 4, 6, 1, 3, 5, 7)
GAIN_ROWS = 16
ROW_STEPS = 1


def mm(a, b, ca=1, cb=0):
    return lax.dot_general(a, b, (((ca,), (cb,)), ((), ())), preferred_element_type=F32)


def shape_of(shape, dtype=BF16):
    return jax.ShapeDtypeStruct(shape, dtype)


def call(kernel, grid, in_specs, out_specs, out_shape, flops, scratch=()):
    return pl.pallas_call(
        kernel,
        out_shape=out_shape,
        grid_spec=pltpu.PrefetchScalarGridSpec(
            num_scalar_prefetch=1,
            grid=grid,
            in_specs=in_specs,
            out_specs=out_specs,
            scratch_shapes=list(scratch),
        ),
        compiler_params=pltpu.CompilerParams(
            dimension_semantics=("arbitrary",) * len(grid), vmem_limit_bytes=VMEM_LIMIT
        ),
        cost_estimate=pl.CostEstimate(flops=1, bytes_accessed=1, transcendentals=0),
    )


def tie(x, *after):
    return lax.optimization_barrier((x, after))[0]


def whole(shape):
    return pl.BlockSpec(shape, lambda i, t: (0,) * len(shape))


def part_at(shape, index):
    return pl.BlockSpec(shape, lambda i, t: (0, index))


def rows_at(rows, cols):
    return pl.BlockSpec((rows, cols), lambda i, t: (i, 0))


def rows_xor(rows, cols):
    return pl.BlockSpec((rows, cols), lambda i, t: (lax.bitwise_xor(i, t[0]), 0))


def model_block(t, p):
    return pl.multiple_of(lax.bitwise_xor(t[1], ORDER[p]) * HEAD, HEAD)


def pack_attn_kernel(kv_heads, group, t, wq, wk, wv, wo, g_attn, g_mlp, g_query, g_key, out):
    n = wq.shape[0]
    for h in range(kv_heads):
        base = h * (group + 2) * HEAD
        mid = base + group * HEAD
        out[:n, base:mid] = wq[:, h * group * HEAD : (h + 1) * group * HEAD]
        out[:n, mid : mid + HEAD] = wk[:, h * HEAD : (h + 1) * HEAD]
        out[:n, mid + HEAD : mid + 2 * HEAD] = wv[:, h * HEAD : (h + 1) * HEAD]
    out[:n, kv_heads * (group + 2) * HEAD :] = wo[...].T
    out[n:, :] = jnp.zeros((GAIN_ROWS, out.shape[1]), BF16)
    m = g_query.shape[1]
    place = lax.broadcasted_iota(jnp.int32, (m, HEAD), 0) + t[1] * m == lax.broadcasted_iota(
        jnp.int32, (m, HEAD), 1
    )
    place = jnp.where(place, 1.0, 0.0).astype(BF16)
    rows = (g_attn[...].astype(F32), g_mlp[...].astype(F32), mm(g_query[...], place), mm(g_key[...], place))
    at = lax.broadcasted_iota(jnp.int32, (GAIN_ROWS, HEAD), 0)
    tile = jnp.zeros((GAIN_ROWS, HEAD), F32)
    for k, row in enumerate(rows):
        tile = jnp.where(at == k, row, tile)
    out[n:, :HEAD] = tile.astype(BF16)


def pack_attn(t, wq, wk, wv, wo, gains, kv_heads, group):
    n = wq.shape[0]
    cols = kv_heads * (group + 2) * HEAD + wo.shape[0]
    args = (wq, wk, wv, wo, *[g[None, :] for g in gains])
    return call(
        functools.partial(pack_attn_kernel, kv_heads, group),
        (1,),
        [whole(a.shape) for a in args],
        whole((n + GAIN_ROWS, cols)),
        shape_of((n + GAIN_ROWS, cols)),
        n * cols,
    )(t, *args)


def pack_rows_kernel(t, x, g, out):
    width = x.shape[1]
    for p in range(width // HEAD):
        at = model_block(t, p)
        out[:, p * HEAD : (p + 1) * HEAD] = x[:, pl.ds(at, HEAD)]
        out[:, width + p * HEAD : width + (p + 1) * HEAD] = g[:, pl.ds(at, HEAD)]


def pack_rows(t, x, g):
    n, width = x.shape
    return call(
        pack_rows_kernel,
        (1,),
        [whole(x.shape), whole(g.shape)],
        whole((n, 2 * width)),
        shape_of((n, 2 * width)),
        n * width,
    )(t, x, g)


def pack_mlp_kernel(t, wg, wu, wd, out):
    ff = wg.shape[1]
    out[:, :ff] = wg[...]
    out[:, ff : 2 * ff] = wu[...]
    out[:, 2 * ff :] = wd[...].T


def pack_mlp(t, wg, wu, wd):
    shape = (wg.shape[0], 3 * wg.shape[1])
    args = (wg, wu, wd)
    return call(
        pack_mlp_kernel,
        (1,),
        [whole(a.shape) for a in args],
        whole(shape),
        shape_of(shape),
        shape[0] * shape[1],
    )(t, *args)


def join(blocks, out):
    n = out.shape[0] // len(blocks)
    for p, b in enumerate(blocks):
        out[p * n : (p + 1) * n, :] = b[:n, :]


def qkv_kernel(nx, nw, packed_gains, kv_heads, group, t, *refs):
    xs, ws = refs[:nx], refs[nx : nx + nw]
    gains_in, cos, sin, normed, packed, raw, gains, w, x = refs[nx + nw :]
    i = pl.program_id(0)

    @pl.when(i == 0)
    def _():
        join(ws, w)
        if packed_gains:
            n = w.shape[0] // nw
            gains[...] = jnp.zeros_like(gains)
            heads = jnp.zeros((GAIN_ROWS, HEAD), F32)
            for p, b in enumerate(ws):
                tile = b[n:, :HEAD].astype(F32)
                gains[0:2, p * n : (p + 1) * n] = tile[0:2]
                heads = heads + tile
            gains[2:4, :HEAD] = heads[2:4]
        else:
            gains[...] = gains_in[...]

    for k in range(nx):

        @pl.when(i == k)
        def _(k=k):
            x[...] = xs[k][...]

    u = x[...].astype(F32)
    r = lax.rsqrt(jnp.mean(u * u, axis=1, keepdims=True) + EPS)
    low = (u * r * gains[0:1, :]).astype(BF16)
    normed[...] = low
    y = mm(low, w[...])
    c = cos[...]
    s = sin[...]
    gq = gains[2:3, :HEAD]
    gk = gains[3:4, :HEAD]
    for h in range(kv_heads):
        base = h * (group + 2) * HEAD
        kept = h * (group + 1) * HEAD
        for j in range(group + 1):
            v = y[:, base + j * HEAD : base + (j + 1) * HEAD]
            raw[:, kept + j * HEAD : kept + (j + 1) * HEAD] = v
            scale = gq if j < group else gk
            v = v * lax.rsqrt(jnp.mean(v * v, axis=1, keepdims=True) + EPS) * scale
            v = v * c + pltpu.roll(v, HEAD // 2, 1) * s
            packed[:, base + j * HEAD : base + (j + 1) * HEAD] = v.astype(BF16)
        end = base + (group + 1) * HEAD
        packed[:, end : end + HEAD] = y[:, end : end + HEAD].astype(BF16)


def qkv_call(t, xs, ws, gains, packed_gains, cos, sin, width, kv_heads, group):
    rows = xs[0].shape[0]
    n = rows * len(xs)
    cols = kv_heads * (group + 2) * HEAD
    kept = kv_heads * (group + 1) * HEAD
    return call(
        functools.partial(qkv_kernel, len(xs), len(ws), packed_gains, kv_heads, group),
        (len(xs),),
        [part_at((rows, width), 0) for _ in xs]
        + [part_at((w.shape[0], cols), 0) for w in ws]
        + [whole(gains.shape), rows_xor(rows, HEAD), rows_xor(rows, HEAD)],
        [rows_at(rows, width), rows_xor(rows, cols), rows_xor(rows, kept), whole((8, width))],
        [
            shape_of((n, width)),
            shape_of((n, cols)),
            shape_of((n, kept), F32),
            shape_of((8, width), F32),
        ],
        2 * n * width * cols,
        [pltpu.VMEM((width, cols), BF16), pltpu.VMEM((rows, width), BF16)],
    )(t, *xs, *ws, gains, cos, sin)


def weights_of(q, k, same, causal):
    e = jnp.exp2(mm(k, q, 1, 1) * EXP2_SCALE)
    keep = same if causal is None else same & causal
    return jnp.where(keep, e, 0.0)


def accumulate(part, acc):
    h = pl.program_id(0)

    @pl.when(h == 0)
    def _():
        acc[...] = part

    @pl.when(h > 0)
    def _():
        acc[...] += part


def split_rows(rows, acc, keep, send):
    for k in range(acc.shape[0] // rows):
        out = send if k % 2 else keep
        at = (k // 2) * rows
        out[at : at + rows, :] = acc[k * rows : (k + 1) * rows, :].astype(BF16)


def attn_forward_kernel(rows, blocks, group, kv_heads, nw, t, packed, seg_col, seg_row, *refs):
    ws = refs[:nw]
    mixed, inv, keep, send, w, acc = refs[nw:]
    causal = lax.broadcasted_iota(jnp.int32, (rows, rows), 0) <= lax.broadcasted_iota(
        jnp.int32, (rows, rows), 1
    )
    kc = group * HEAD
    join(ws, w)
    for i in range(blocks):
        lo = i * rows
        at = pl.multiple_of(lax.bitwise_xor(i, t[0]) * rows, rows)
        sq = seg_row[:, lo : lo + rows]
        for j in range(group):
            q = packed[lo : lo + rows, j * HEAD : (j + 1) * HEAD]
            parts = []
            total = jnp.zeros((1, rows), F32)
            for b in range(i + 1):
                k = packed[b * rows : (b + 1) * rows, kc : kc + HEAD]
                same = seg_col[b * rows : (b + 1) * rows, :] == sq
                e = weights_of(q, k, same, causal if b == i else None)
                total = total + jnp.sum(e, axis=0, keepdims=True)
                parts.append(e)
            rec = 1.0 / total
            inv[0, j : j + 1, lo : lo + rows] = rec
            out = jnp.zeros((rows, HEAD), F32)
            for b in range(i + 1):
                v = packed[b * rows : (b + 1) * rows, kc + HEAD : kc + 2 * HEAD]
                out = out + mm((parts[b] * rec).astype(BF16), v, 0, 0)
            mixed[pl.ds(at, rows), j * HEAD : (j + 1) * HEAD] = out.astype(BF16)
    accumulate(mm(mixed[...], w[...], 1, 1), acc)

    @pl.when(pl.program_id(0) == kv_heads - 1)
    def _():
        split_rows(rows, acc, keep, send)


def by_head(n, width, first=0):
    return pl.BlockSpec((n, width), lambda h, t: (0, first + h))


def attn_forward(t, packed, seg_col, seg_row, w_o, first, rows, width, kv_heads, group):
    n = packed.shape[0]
    q_cols = group * HEAD
    return call(
        functools.partial(attn_forward_kernel, rows, n // rows, group, kv_heads, len(w_o)),
        (kv_heads,),
        [by_head(n, q_cols + 2 * HEAD), whole(seg_col.shape), whole(seg_row.shape)]
        + [by_head(w.shape[0], q_cols, first) for w in w_o],
        [
            by_head(n, q_cols),
            pl.BlockSpec((1, 8, n), lambda h, t: (h, 0, 0)),
            whole((n // 2, width)),
            whole((n // 2, width)),
        ],
        [
            shape_of((n, kv_heads * q_cols)),
            shape_of((kv_heads, 8, n), F32),
            shape_of((n // 2, width)),
            shape_of((n // 2, width)),
        ],
        kv_heads * group * n * n * HEAD * 4,
        [pltpu.VMEM((width, q_cols), BF16), pltpu.VMEM((n, width), F32)],
    )(t, packed, seg_col, seg_row, *w_o)


def head_back(e, u, cos, sin, gain):
    e = e * cos - pltpu.roll(e, HEAD // 2, 1) * sin
    r = lax.rsqrt(jnp.mean(u * u, axis=1, keepdims=True) + EPS)
    ur = u * r
    dgain = jnp.sum(e * ur, axis=0, keepdims=True)
    ec = e * gain
    du = r * (ec - ur * jnp.mean(ur * ec, axis=1, keepdims=True))
    return du, dgain


def attn_backward_kernel(rows, blocks, group, kv_heads, nw, t, *refs):
    packed, seg_col, seg_row, inv, raw, cos, sin, gains = refs[:8]
    refs = refs[8:]
    branch, refs = refs[:blocks], refs[blocks:]
    xs, refs = refs[:blocks], refs[blocks:]
    w_os, refs = refs[:nw], refs[nw:]
    w_qkvs, refs = refs[:nw], refs[nw:]
    dpacked, dgain, keep, send, dgain_x, dk, dv, dmix, w_o, w_qkv, acc = refs
    causal = lax.broadcasted_iota(jnp.int32, (rows, rows), 0) <= lax.broadcasted_iota(
        jnp.int32, (rows, rows), 1
    )
    kc = group * HEAD
    gq = gains[2:3, :HEAD]
    gk = gains[3:4, :HEAD]
    join(w_os, w_o)
    join(w_qkvs, w_qkv)
    for k in range(blocks):
        dmix[k * rows : (k + 1) * rows, :] = mm(branch[k][...], w_o[...]).astype(BF16)
    dk[...] = jnp.zeros_like(dk)
    dv[...] = jnp.zeros_like(dv)
    dgain[...] = jnp.zeros_like(dgain)
    for i in range(blocks):
        lo = i * rows
        at = pl.multiple_of(lax.bitwise_xor(i, t[0]) * rows, rows)
        sq = seg_row[:, lo : lo + rows]
        for j in range(group):
            q = packed[lo : lo + rows, j * HEAD : (j + 1) * HEAD]
            do = dmix[pl.ds(at, rows), j * HEAD : (j + 1) * HEAD]
            rec = inv[0, j : j + 1, lo : lo + rows]
            probs = []
            dprobs = []
            delta = jnp.zeros((1, rows), F32)
            for b in range(i + 1):
                here = slice(b * rows, (b + 1) * rows)
                k = packed[here, kc : kc + HEAD]
                v = packed[here, kc + HEAD : kc + 2 * HEAD]
                same = seg_col[here, :] == sq
                p = weights_of(q, k, same, causal if b == i else None) * rec
                dp = mm(v, do, 1, 1)
                delta = delta + jnp.sum(p * dp, axis=0, keepdims=True)
                dv[here, :] += mm(p.astype(BF16), do)
                probs.append(p)
                dprobs.append(dp)
            dq = jnp.zeros((rows, HEAD), F32)
            for b in range(i + 1):
                here = slice(b * rows, (b + 1) * rows)
                k = packed[here, kc : kc + HEAD]
                ds = (probs[b] * (dprobs[b] - delta)).astype(BF16)
                dk[here, :] += mm(ds, q)
                dq = dq + mm(ds, k, 0, 0)
            du, dg = head_back(
                dq * SCALE,
                raw[lo : lo + rows, j * HEAD : (j + 1) * HEAD],
                cos[lo : lo + rows, :],
                sin[lo : lo + rows, :],
                gq,
            )
            dgain[0, 0:1, :] += dg
            dpacked[pl.ds(at, rows), j * HEAD : (j + 1) * HEAD] = du.astype(BF16)
    for i in range(blocks):
        here = slice(i * rows, (i + 1) * rows)
        at = pl.multiple_of(lax.bitwise_xor(i, t[0]) * rows, rows)
        du, dg = head_back(
            dk[here, :] * SCALE, raw[here, kc : kc + HEAD], cos[here, :], sin[here, :], gk
        )
        dgain[0, 1:2, :] += dg
        dpacked[pl.ds(at, rows), kc : kc + HEAD] = du.astype(BF16)
        dpacked[pl.ds(at, rows), kc + HEAD : kc + 2 * HEAD] = dv[here, :].astype(BF16)
    accumulate(mm(dpacked[...], w_qkv[...], 1, 1), acc)

    @pl.when(pl.program_id(0) == kv_heads - 1)
    def _():
        total = jnp.zeros((1, acc.shape[1]), F32)
        for k in range(blocks):
            u = xs[k][...].astype(F32)
            ur = u * lax.rsqrt(jnp.mean(u * u, axis=1, keepdims=True) + EPS)
            total = total + jnp.sum(acc[k * rows : (k + 1) * rows, :] * ur, axis=0, keepdims=True)
        dgain_x[...] = jnp.broadcast_to(total, dgain_x.shape)
        split_rows(rows, acc, keep, send)


def attn_backward(
    t, packed, seg_col, seg_row, inv, raw, cos, sin, gains, branch, xs, w_o, first, w_qkv, width, kv_heads, group
):
    n = packed.shape[0]
    rows = xs[0].shape[0]
    q_cols = group * HEAD
    cols = q_cols + 2 * HEAD
    return call(
        functools.partial(attn_backward_kernel, rows, n // rows, group, kv_heads, len(w_o)),
        (kv_heads,),
        [
            by_head(n, cols),
            whole(seg_col.shape),
            whole(seg_row.shape),
            pl.BlockSpec((1, 8, n), lambda h, t: (h, 0, 0)),
            by_head(n, q_cols + HEAD),
            whole(cos.shape),
            whole(sin.shape),
            whole(gains.shape),
        ]
        + [whole(b.shape) for b in branch]
        + [part_at((rows, width), 0) for _ in xs]
        + [by_head(w.shape[0], q_cols, first) for w in w_o]
        + [by_head(w.shape[0], cols) for w in w_qkv],
        [
            by_head(n, cols),
            pl.BlockSpec((1, 8, HEAD), lambda h, t: (h, 0, 0)),
            whole((n // 2, width)),
            whole((n // 2, width)),
            whole((8, width)),
        ],
        [
            shape_of(packed.shape),
            shape_of((kv_heads, 8, HEAD), F32),
            shape_of((n // 2, width)),
            shape_of((n // 2, width)),
            shape_of((8, width), F32),
        ],
        kv_heads * group * n * n * HEAD * 10,
        [
            pltpu.VMEM((n, HEAD), F32),
            pltpu.VMEM((n, HEAD), F32),
            pltpu.VMEM((n, q_cols), BF16),
            pltpu.VMEM((width, q_cols), BF16),
            pltpu.VMEM((width, cols), BF16),
            pltpu.VMEM((n, width), F32),
        ],
    )(t, packed, seg_col, seg_row, inv, raw, cos, sin, gains, *branch, *xs, *w_o, *w_qkv)


def join_in_order(t, reorder, block, out):
    if not reorder:
        out[...] = block[...]
        return
    for p in range(out.shape[0] // HEAD):
        out[p * HEAD : (p + 1) * HEAD, :] = block[pl.ds(model_block(t, p), HEAD), :]


def mlp_kernel(ff, nx, reorder, t, *refs):
    xs, refs = refs[:nx], refs[nx:]
    gs, refs = refs[:nx], refs[nx:]
    w_gu, w_d, *refs = refs
    act, dgu, x_out, g_out, dx_keep, dx_send, out_keep, out_send, w, wd, x, g = refs
    i = pl.program_id(0)

    @pl.when(i == 0)
    def _():
        join_in_order(t, reorder, w_gu, w)
        join_in_order(t, reorder, w_d, wd)

    for k in range(nx):

        @pl.when(i == k)
        def _(k=k):
            x[...] = xs[k][...]
            g[...] = gs[k][...]
            store_columns(t, reorder, xs[k][...], x_out)
            g_out[...] = gs[k][...]

    y = mm(x[...], w[...])
    gate = y[:, :ff]
    up = y[:, ff:]
    sig = 1.0 / (1.0 + jnp.exp(-gate))
    silu = gate * sig
    a = (silu * up).astype(BF16)
    act[...] = a
    da = mm(g[...], wd[...])
    dgu[:, :ff] = (da * up * sig * (1.0 + gate * (1.0 - sig))).astype(BF16)
    dgu[:, ff:] = (da * silu).astype(BF16)
    dx = mm(dgu[...], w[...], 1, 1).astype(BF16)
    out = mm(a, wd[...], 1, 1).astype(BF16)

    @pl.when(lax.rem(i, 2) == 0)
    def _():
        dx_keep[...] = dx
        out_keep[...] = out

    @pl.when(lax.rem(i, 2) == 1)
    def _():
        dx_send[...] = dx
        out_send[...] = out


def mlp_call(t, reorder, xs, gs, g_index, w_gu, w_d, d_index, ff, width):
    rows = xs[0].shape[0]
    n = rows * len(xs)
    halves = pl.BlockSpec((rows, width), lambda i, t: (lax.div(i, 2), 0))
    return call(
        functools.partial(mlp_kernel, ff, len(xs), reorder),
        (len(xs),),
        [whole(x.shape) for x in xs]
        + [part_at((rows, width), g_index) for _ in gs]
        + [part_at((width, 2 * ff), 0), part_at((width, ff), d_index)],
        [rows_at(rows, ff), rows_at(rows, 2 * ff)] + [rows_at(rows, width)] * 2 + [halves] * 4,
        [shape_of((n, ff)), shape_of((n, 2 * ff))]
        + [shape_of((n, width))] * 2
        + [shape_of((n // 2, width))] * 4,
        2 * n * width * ff * 6,
        [
            pltpu.VMEM((width, 2 * ff), BF16),
            pltpu.VMEM((width, ff), BF16),
            pltpu.VMEM((rows, width), BF16),
            pltpu.VMEM((rows, width), BF16),
        ],
    )(t, *xs, *gs, w_gu, w_d)


def sum_of(parts):
    total = parts[0][...].astype(F32)
    for p in parts[1:]:
        total = total + p[...].astype(F32)
    return total


def hidden_kernel(n_parts, t, *refs):
    parts = refs[:n_parts]
    x, gains, hidden, normed = refs[n_parts:]
    h = x[...].astype(F32) + sum_of(parts)
    hidden[...] = h
    r = lax.rsqrt(jnp.mean(h * h, axis=1, keepdims=True) + EPS)
    normed[...] = (h * r * gains[1:2, :]).astype(BF16)


def row_tile(rows, width, index=0):
    return pl.BlockSpec((rows // ROW_STEPS, width), lambda i, t: (i, index))


def hidden_call(t, parts, x, gains, rows, width):
    spec = row_tile(rows, width)
    return call(
        functools.partial(hidden_kernel, len(parts)),
        (ROW_STEPS,),
        [spec for _ in parts] + [spec, whole(gains.shape)],
        [spec, spec],
        [shape_of((rows, width), F32), shape_of((rows, width))],
        rows * width * 8,
    )(t, *parts, x, gains)


def norm_back(e, u, gain):
    r = lax.rsqrt(jnp.mean(u * u, axis=1, keepdims=True) + EPS)
    ur = u * r
    ec = e * gain
    return r * (ec - ur * jnp.mean(ur * ec, axis=1, keepdims=True)), jnp.sum(e * ur, axis=0, keepdims=True)


def d_hidden_kernel(n_parts, t, *refs):
    parts = refs[:n_parts]
    hidden, g, gains, d_hidden, branch, d_gain = refs[n_parts:]
    du, dg = norm_back(sum_of(parts), hidden[...], gains[1:2, :])
    d = g[...].astype(F32) + du
    d_hidden[...] = d
    branch[...] = d.astype(BF16)
    accumulate(jnp.broadcast_to(dg, d_gain.shape), d_gain)


def d_hidden_call(t, parts, hidden, g, g_index, gains, rows, width):
    spec = row_tile(rows, width)
    return call(
        functools.partial(d_hidden_kernel, len(parts)),
        (ROW_STEPS,),
        [spec for _ in parts] + [spec, row_tile(rows, width, g_index), whole(gains.shape)],
        [spec, spec, whole((8, width))],
        [shape_of((rows, width), F32), shape_of((rows, width)), shape_of((8, width), F32)],
        rows * width * 12,
    )(t, *parts, hidden, g, gains)


def store_columns(t, reorder, value, out):
    if not reorder:
        out[...] = value
        return
    for p in range(value.shape[1] // HEAD):
        out[:, pl.ds(model_block(t, p), HEAD)] = value[:, p * HEAD : (p + 1) * HEAD]


def activations_kernel(n_parts, reorder, t, *refs):
    parts = refs[:n_parts]
    hidden, out = refs[n_parts:]
    store_columns(t, reorder, (hidden[...] + sum_of(parts)).astype(BF16), out)


def activations_call(t, reorder, parts, hidden, rows, width):
    spec = row_tile(rows, width)
    return call(
        functools.partial(activations_kernel, len(parts), reorder),
        (ROW_STEPS,),
        [spec for _ in parts] + [spec],
        spec,
        shape_of((rows, width)),
        rows * width * 2,
    )(t, *parts, hidden)


def d_tokens_kernel(n_parts, reorder, t, *refs):
    parts = refs[:n_parts]
    x, d_hidden, gains, out = refs[n_parts:]
    du, _ = norm_back(sum_of(parts), x[...].astype(F32), gains[0:1, :])
    store_columns(t, reorder, d_hidden[...] + du, out)


def d_tokens_call(t, reorder, parts, x, d_hidden, gains, rows, width):
    spec = row_tile(rows, width)
    return call(
        functools.partial(d_tokens_kernel, len(parts), reorder),
        (ROW_STEPS,),
        [spec for _ in parts] + [spec, spec, whole(gains.shape)],
        spec,
        shape_of((rows, width), F32),
        rows * width * 12,
    )(t, *parts, x, d_hidden, gains)


def outer_half(left, right, half):
    m = left.shape[1] // 2
    return mm(left[:, half * m : (half + 1) * m], right, 0, 0).astype(BF16)


def shard_of(parts):
    total = parts[0].astype(F32)
    for p in parts[1:]:
        total = total + p.astype(F32)
    return total


def unpack_heads(kv_heads, group, w):
    q, k, v = [], [], []
    for h in range(kv_heads):
        base = h * (group + 2) * HEAD
        mid = base + group * HEAD
        q.append(w[:, base:mid])
        k.append(w[:, mid : mid + HEAD])
        v.append(w[:, mid + HEAD : mid + 2 * HEAD])
    join = lambda parts: jnp.concatenate(parts, axis=1)
    return join(q), join(k), join(v)


def gain_rows_kernel(t, d_attn, d_mlp, d_heads, out):
    heads = jnp.sum(d_heads[...], axis=0)
    at = lax.broadcasted_iota(jnp.int32, (GAIN_ROWS, 4 * HEAD), 0)
    for p in range(d_attn.shape[1] // HEAD):
        here = slice(p * HEAD, (p + 1) * HEAD)
        row = jnp.concatenate([d_attn[0:1, here], d_mlp[0:1, here], heads[0:1], heads[1:2]], axis=1)
        rows = slice(p * GAIN_ROWS, (p + 1) * GAIN_ROWS)
        out[rows, : 4 * HEAD] = jnp.where(at == 0, row, 0.0).astype(BF16)
        out[rows, 4 * HEAD :] = jnp.zeros((GAIN_ROWS, out.shape[1] - 4 * HEAD), BF16)


def gain_rows(t, d_attn, d_mlp, d_heads, cols):
    args = (d_attn, d_mlp, d_heads)
    rows = d_attn.shape[1] // HEAD * GAIN_ROWS
    return call(
        gain_rows_kernel,
        (1,),
        [whole(a.shape) for a in args],
        whole((rows, cols)),
        shape_of((rows, cols)),
        rows * HEAD,
    )(t, *args)


def pair_sum_kernel(t, keep, rows, got, *outs):
    n = keep.shape[0] // len(outs)
    for z, out in enumerate(outs):
        here = slice(z * n, (z + 1) * n)
        low = slice(z * GAIN_ROWS, (z + 1) * GAIN_ROWS)
        there = slice(keep.shape[0] + z * GAIN_ROWS, keep.shape[0] + (z + 1) * GAIN_ROWS)
        out[:n, :] = (keep[here, :].astype(F32) + got[here, :].astype(F32)).astype(out.dtype)
        out[n:, :] = (rows[low, :].astype(F32) + got[there, :].astype(F32)).astype(out.dtype)


def pair_sum(t, keep, rows, got, parts):
    m, cols = keep.shape
    n = m // parts + GAIN_ROWS
    return call(
        pair_sum_kernel,
        (1,),
        [whole(keep.shape), whole(rows.shape), whole(got.shape)],
        [whole((n, cols)) for _ in range(parts)],
        [shape_of((n, cols), F32 if z == 0 else BF16) for z in range(parts)],
        m * cols,
    )(t, keep, rows, got)


def xor_pairs(size, bits):
    return [(i, i ^ bits) for i in range(size)]


class Links:
    def __init__(self, dp, tensor):
        self.dp, self.tensor = dp, tensor
        self.direct = (dp, tensor) == (8, 4)
        self.d = lax.axis_index("dp")
        self.t = lax.axis_index("tensor")

    def over_dp(self, x, bits):
        return lax.ppermute(x, "dp", xor_pairs(self.dp, bits))

    def over_tensor(self, x, bits):
        return lax.ppermute(x, "tensor", xor_pairs(self.tensor, bits))

    def offsets(self):
        if self.direct:
            return jnp.stack([self.t, self.d])
        return jnp.zeros((2,), jnp.int32)

    def gather_dp(self, x):
        if not self.direct:
            return [lax.all_gather(x, "dp", axis=0, tiled=True)]
        own = self.gather_z(x)
        return own + [self.over_dp(b, 1) for b in own]

    def gather_z(self, x):
        return [x] + [self.over_dp(x, 2 * z) for z in (1, 2, 3)]

    def send_half(self, left, right):
        send = outer_half(left, right, 1)
        if self.direct:
            send = self.over_dp(send, 1)
        return send, outer_half(left, right, 0)

    def send_quarters(self, got, keep):
        if not self.direct:
            both = jnp.concatenate([keep, got], axis=0)
            return [lax.psum_scatter(both, "dp", scatter_dimension=0, tiled=True)]
        n = keep.shape[0] // 4
        part = lambda z: keep[z * n : (z + 1) * n].astype(F32) + got[z * n : (z + 1) * n].astype(F32)
        return [part(0)] + [self.over_dp(part(z).astype(BF16), 2 * z) for z in (1, 2, 3)]

    def gather_tensor(self, x, *after):
        if not self.direct:
            full = lax.all_gather(x, "tensor", axis=0, tiled=True)
            return jnp.split(full, self.tensor, axis=0)
        far = self.over_tensor(x, 2)
        return [x, self.over_tensor(x, 1), far, self.over_tensor(tie(far, *after) if after else far, 1)]

    def scatter_tensor(self, keep, send):
        rows = 2 * keep.shape[0] // self.tensor
        if not self.direct:
            blocks = []
            for k in range(self.tensor // 2):
                blocks += [keep[k * rows : (k + 1) * rows], send[k * rows : (k + 1) * rows]]
            full = jnp.concatenate(blocks, axis=0)
            return [lax.psum_scatter(full, "tensor", scatter_dimension=0, tiled=True)]
        got = self.over_tensor(send, 1)
        far = keep[rows:].astype(F32) + got[rows:].astype(F32)
        return [keep, got, self.over_tensor(far.astype(BF16), 2)]


def rope_tables(offsets):
    frequency = ROPE_BASE ** (-(2.0 * jnp.arange(HEAD // 2, dtype=F32)) / HEAD)
    angles = offsets.astype(F32)[:, None] * frequency[None, :]
    cos, sin = jnp.cos(angles), jnp.sin(angles)
    return jnp.concatenate([cos, cos], axis=1), jnp.concatenate([-sin, sin], axis=1)


def pack_heads(wq, wk, wv, group):
    parts = []
    for h in range(wk.shape[1] // HEAD):
        parts += [
            wq[:, h * group * HEAD : (h + 1) * group * HEAD],
            wk[:, h * HEAD : (h + 1) * HEAD],
            wv[:, h * HEAD : (h + 1) * HEAD],
        ]
    return jnp.concatenate(parts, axis=1)


def body(
    dp,
    tensor,
    tokens,
    segment_ids,
    positions,
    w_query,
    key_projection,
    value_projection,
    w_out,
    w_gate,
    w_up,
    w_down,
    gain_attn,
    gain_mlp,
    gain_query,
    gain_key,
    cotangent,
):
    links = Links(dp, tensor)
    direct = links.direct
    rows, width = tokens.shape
    kv_heads = key_projection.shape[1] // HEAD
    group = w_query.shape[1] // key_projection.shape[1]
    q_cols = group * HEAD
    ff = w_gate.shape[1]
    head_part = HEAD // dp
    t = links.offsets()

    if direct:
        w_attn = pack_attn(
            t,
            w_query,
            key_projection,
            value_projection,
            w_out,
            (gain_attn, gain_mlp, gain_query, gain_key),
            kv_heads,
            group,
        )
        both = pack_rows(t, tie(tokens, w_attn), cotangent)
        w_mlp = pack_mlp(t, tie(w_gate, both), w_up, w_down)
        attn_near = links.gather_z(w_attn)
        attn_far = links.over_dp(w_attn, 1)
        beside = links.over_tensor(both, 1)
        far = links.over_tensor(both, 2)
        across = tie(far, attn_far, attn_near[1], attn_near[2])
        rows_all = [both, beside, far, links.over_tensor(across, 1)]
        w_mlp = tie(w_mlp, (far, attn_far, attn_near[1], attn_near[2]))
        w_attn = attn_near + [attn_far] + [links.over_dp(b, 1) for b in attn_near[1:]]
        w_qkv, w_o, o_index = w_attn, w_attn, kv_heads * (group + 2) * HEAD // q_cols
        w_gu = w_d = lax.all_gather(w_mlp, "dp", axis=0, tiled=True)
        d_index = 2
        gains = jnp.zeros((8, width), F32)
    else:
        w_qkv = links.gather_dp(pack_heads(w_query, key_projection, value_projection, group))
        w_o = links.gather_dp(w_out.T)
        w_gu = links.gather_dp(jnp.concatenate([w_gate, w_up], axis=1))[0]
        w_d = links.gather_dp(w_down.T)[0]
        d_index, o_index = 0, 0
        row = lambda g: jnp.pad(g, (0, width - g.shape[0]))[None, :].astype(F32)
        whole_gain = lambda g: row(lax.all_gather(g, "dp", axis=0, tiled=True))
        gains = jnp.concatenate(
            [whole_gain(g) for g in (gain_attn, gain_mlp, gain_query, gain_key)]
            + [jnp.zeros((4, width), F32)],
            axis=0,
        )
        rows_all = links.gather_tensor(jnp.concatenate([tokens, cotangent], axis=1))
    own = rows_all[0] if direct else jnp.concatenate([tokens, cotangent], axis=1)

    cos, sin = rope_tables(positions[0])
    seg_row = segment_ids
    seg_col = segment_ids.reshape(-1, 1)

    normed, packed, raw, gains = qkv_call(
        t, rows_all, w_qkv, gains, direct, cos, sin, width, kv_heads, group
    )
    mixed, inv, keep, send = attn_forward(
        t, packed, seg_col, seg_row, w_o, o_index, rows, width, kv_heads, group
    )
    parts = links.scatter_tensor(keep, send)
    hidden, normed_mlp = hidden_call(t, parts, own, gains, rows, width)
    normed_mlp = links.gather_tensor(normed_mlp)
    act, d_gu, normed_mlp, cot, dx_keep, dx_send, out_keep, out_send = mlp_call(
        t, direct, normed_mlp, rows_all, 1, w_gu, w_d, d_index, ff, width
    )
    parts = links.scatter_tensor(dx_keep, dx_send)
    gu_sum = mm(normed_mlp, tie(d_gu, parts[:2]), 0, 0).astype(BF16)
    gu = lax.psum_scatter(gu_sum, "dp", scatter_dimension=0, tiled=True)
    d_hidden, branch, d_gain_mlp = d_hidden_call(
        t, tie(parts, gu_sum), hidden, own, 1, gains, rows, width
    )
    down = links.send_half(cot, tie(act, branch))
    branch = links.gather_tensor(branch, down[1])
    out_parts = links.scatter_tensor(out_keep, tie(out_send, branch))
    out = links.send_half(jnp.concatenate(branch, axis=0), mixed)
    d_packed, d_gain_heads, keep, send, d_gain_attn = tie(
        attn_backward(
            t, packed, seg_col, seg_row, inv, raw, cos, sin, gains, branch, rows_all, w_o, o_index, w_qkv,
            width, kv_heads, group,
        ),
        out[0],
        down[0],
        out_parts,
    )
    if direct:
        tails = gain_rows(t, d_gain_attn, d_gain_mlp, d_gain_heads, d_packed.shape[1])
        half = tails.shape[0] // 2
        send_qkv = jnp.concatenate([outer_half(normed, d_packed, 1), tails[half:]], axis=0)
        got = links.over_dp(send_qkv, 1)
        parts = links.scatter_tensor(keep, send)
        out, down = tie((out, down), parts[:2])
        out = links.send_quarters(*out)
        down = links.send_quarters(*down)
        qkv = pair_sum(t, outer_half(normed, d_packed, 0), tails[:half], tie(got, out[1:], down[1:], gu), 4)
        qkv = [qkv[0]] + [links.over_dp(qkv[z], 2 * z) for z in (1, 2, 3)]
    else:
        qkv = links.send_quarters(*links.send_half(normed, d_packed))
        out = links.send_quarters(*out)
        down = links.send_quarters(*down)
        parts = links.scatter_tensor(keep, send)
    d_tokens = d_tokens_call(t, direct, parts, own, d_hidden, gains, rows, width)
    activations = activations_call(t, direct, out_parts, hidden, rows, width)
    grad_down = shard_of(down).T
    grad_gate, grad_up = gu[:, :ff].astype(F32), gu[:, ff:].astype(F32)
    grad_out = shard_of(out).T
    n = width // dp
    qkv = shard_of(qkv)
    grad_query, grad_key, grad_value = unpack_heads(kv_heads, group, qkv[:n])
    if direct:
        sums = qkv[n : n + 1, : 4 * HEAD]
        sums = sums + links.over_tensor(sums, 1)
        sums = (sums + links.over_tensor(sums, 2)).reshape(4, HEAD)
        sum_attn, sum_mlp, sum_query, sum_key = sums[0], sums[1], sums[2], sums[3]
    else:
        heads = jnp.sum(d_gain_heads, axis=0)
        sum_attn, sum_mlp, sum_query, sum_key = lax.psum(
            (d_gain_attn[0], d_gain_mlp[0], heads[0], heads[1]), ("dp", "tensor")
        )
        sum_attn = lax.dynamic_slice_in_dim(sum_attn, links.d * n, n, 0)
        sum_mlp = lax.dynamic_slice_in_dim(sum_mlp, links.d * n, n, 0)
    shard = lambda v: lax.dynamic_slice_in_dim(v, links.d * head_part, head_part, 0)
    return (
        activations,
        d_tokens,
        grad_query,
        grad_key,
        grad_value,
        grad_out,
        grad_gate,
        grad_up,
        grad_down,
        sum_attn,
        sum_mlp,
        shard(sum_query),
        shard(sum_key),
    )


def solution(mesh):
    tokens = P(("dp", "tensor"), None)
    by_rows = P("dp", "tensor")
    by_columns = P("tensor", "dp")
    sequence = P("dp", None)
    gain = P("dp")
    return jax.shard_map(
        functools.partial(body, mesh.shape["dp"], mesh.shape["tensor"]),
        mesh=mesh,
        in_specs=(
            tokens,
            sequence,
            sequence,
            by_rows,
            by_rows,
            by_rows,
            by_columns,
            by_rows,
            by_rows,
            by_columns,
            gain,
            gain,
            gain,
            gain,
            tokens,
        ),
        out_specs=(
            tokens,
            tokens,
            by_rows,
            by_rows,
            by_rows,
            by_columns,
            by_rows,
            by_rows,
            by_columns,
            gain,
            gain,
            gain,
            gain,
        ),
        check_vma=False,
    )
```

```python
import functools

import jax
import jax.numpy as jnp
from jax import lax
from jax.experimental import pallas as pl
from jax.experimental.pallas import tpu as pltpu
from jax.sharding import PartitionSpec as P

HEAD = 128
EPS = 1e-06
ROPE_BASE = 1000000.0
SCALE = HEAD ** (-0.5)
EXP2_SCALE = SCALE * 1.4426950408889634
F32 = jnp.float32
BF16 = jnp.bfloat16
VMEM_LIMIT = 60 * 1024 * 1024
ORDER = (0, 2, 4, 6, 1, 3, 5, 7)
GAIN_ROWS = 16
ROW_STEPS = 1


def mm(a, b, ca=1, cb=0):
    return lax.dot_general(a, b, (((ca,), (cb,)), ((), ())), preferred_element_type=F32)


def shape_of(shape, dtype=BF16):
    return jax.ShapeDtypeStruct(shape, dtype)


def call(kernel, grid, in_specs, out_specs, out_shape, flops, scratch=()):
    return pl.pallas_call(
        kernel,
        out_shape=out_shape,
        grid_spec=pltpu.PrefetchScalarGridSpec(
            num_scalar_prefetch=1,
            grid=grid,
            in_specs=in_specs,
            out_specs=out_specs,
            scratch_shapes=list(scratch),
        ),
        compiler_params=pltpu.CompilerParams(
            dimension_semantics=("arbitrary",) * len(grid), vmem_limit_bytes=VMEM_LIMIT
        ),
        cost_estimate=pl.CostEstimate(flops=1, bytes_accessed=1, transcendentals=0),
    )


def tie(x, *after):
    return lax.optimization_barrier((x, after))[0]


def whole(shape):
    return pl.BlockSpec(shape, lambda i, t: (0,) * len(shape))


def part_at(shape, index):
    return pl.BlockSpec(shape, lambda i, t: (0, index))


def rows_at(rows, cols):
    return pl.BlockSpec((rows, cols), lambda i, t: (i, 0))


def rows_xor(rows, cols):
    return pl.BlockSpec((rows, cols), lambda i, t: (lax.bitwise_xor(i, t[0]), 0))


def model_block(t, p):
    return pl.multiple_of(lax.bitwise_xor(t[1], ORDER[p]) * HEAD, HEAD)


def pack_attn_kernel(kv_heads, group, t, wq, wk, wv, wo, g_attn, g_mlp, g_query, g_key, out):
    n = wq.shape[0]
    for h in range(kv_heads):
        base = h * (group + 2) * HEAD
        mid = base + group * HEAD
        out[:n, base:mid] = wq[:, h * group * HEAD : (h + 1) * group * HEAD]
        out[:n, mid : mid + HEAD] = wk[:, h * HEAD : (h + 1) * HEAD]
        out[:n, mid + HEAD : mid + 2 * HEAD] = wv[:, h * HEAD : (h + 1) * HEAD]
    out[:n, kv_heads * (group + 2) * HEAD :] = wo[...].T
    out[n:, :] = jnp.zeros((GAIN_ROWS, out.shape[1]), BF16)
    m = g_query.shape[1]
    place = lax.broadcasted_iota(jnp.int32, (m, HEAD), 0) + t[1] * m == lax.broadcasted_iota(
        jnp.int32, (m, HEAD), 1
    )
    place = jnp.where(place, 1.0, 0.0).astype(BF16)
    rows = (g_attn[...].astype(F32), g_mlp[...].astype(F32), mm(g_query[...], place), mm(g_key[...], place))
    at = lax.broadcasted_iota(jnp.int32, (GAIN_ROWS, HEAD), 0)
    tile = jnp.zeros((GAIN_ROWS, HEAD), F32)
    for k, row in enumerate(rows):
        tile = jnp.where(at == k, row, tile)
    out[n:, :HEAD] = tile.astype(BF16)


def pack_attn(t, wq, wk, wv, wo, gains, kv_heads, group):
    n = wq.shape[0]
    cols = kv_heads * (group + 2) * HEAD + wo.shape[0]
    args = (wq, wk, wv, wo, *[g[None, :] for g in gains])
    return call(
        functools.partial(pack_attn_kernel, kv_heads, group),
        (1,),
        [whole(a.shape) for a in args],
        whole((n + GAIN_ROWS, cols)),
        shape_of((n + GAIN_ROWS, cols)),
        n * cols,
    )(t, *args)


def pack_rows_kernel(t, x, g, out):
    width = x.shape[1]
    for p in range(width // HEAD):
        at = model_block(t, p)
        out[:, p * HEAD : (p + 1) * HEAD] = x[:, pl.ds(at, HEAD)]
        out[:, width + p * HEAD : width + (p + 1) * HEAD] = g[:, pl.ds(at, HEAD)]


def pack_rows(t, x, g):
    n, width = x.shape
    return call(
        pack_rows_kernel,
        (1,),
        [whole(x.shape), whole(g.shape)],
        whole((n, 2 * width)),
        shape_of((n, 2 * width)),
        n * width,
    )(t, x, g)


def pack_mlp_kernel(t, wg, wu, wd, out):
    ff = wg.shape[1]
    out[:, :ff] = wg[...]
    out[:, ff : 2 * ff] = wu[...]
    out[:, 2 * ff :] = wd[...].T


def pack_mlp(t, wg, wu, wd):
    shape = (wg.shape[0], 3 * wg.shape[1])
    args = (wg, wu, wd)
    return call(
        pack_mlp_kernel,
        (1,),
        [whole(a.shape) for a in args],
        whole(shape),
        shape_of(shape),
        shape[0] * shape[1],
    )(t, *args)


def join(blocks, out):
    n = out.shape[0] // len(blocks)
    for p, b in enumerate(blocks):
        out[p * n : (p + 1) * n, :] = b[:n, :]


def qkv_kernel(nx, nw, packed_gains, kv_heads, group, t, *refs):
    xs, ws = refs[:nx], refs[nx : nx + nw]
    gains_in, cos, sin, normed, packed, raw, gains, w, x = refs[nx + nw :]
    i = pl.program_id(0)

    @pl.when(i == 0)
    def _():
        join(ws, w)
        if packed_gains:
            n = w.shape[0] // nw
            gains[...] = jnp.zeros_like(gains)
            heads = jnp.zeros((GAIN_ROWS, HEAD), F32)
            for p, b in enumerate(ws):
                tile = b[n:, :HEAD].astype(F32)
                gains[0:2, p * n : (p + 1) * n] = tile[0:2]
                heads = heads + tile
            gains[2:4, :HEAD] = heads[2:4]
        else:
            gains[...] = gains_in[...]

    for k in range(nx):

        @pl.when(i == k)
        def _(k=k):
            x[...] = xs[k][...]

    u = x[...].astype(F32)
    r = lax.rsqrt(jnp.mean(u * u, axis=1, keepdims=True) + EPS)
    low = (u * r * gains[0:1, :]).astype(BF16)
    normed[...] = low
    y = mm(low, w[...])
    c = cos[...]
    s = sin[...]
    gq = gains[2:3, :HEAD]
    gk = gains[3:4, :HEAD]
    for h in range(kv_heads):
        base = h * (group + 2) * HEAD
        kept = h * (group + 1) * HEAD
        for j in range(group + 1):
            v = y[:, base + j * HEAD : base + (j + 1) * HEAD]
            raw[:, kept + j * HEAD : kept + (j + 1) * HEAD] = v
            scale = gq if j < group else gk
            v = v * lax.rsqrt(jnp.mean(v * v, axis=1, keepdims=True) + EPS) * scale
            v = v * c + pltpu.roll(v, HEAD // 2, 1) * s
            packed[:, base + j * HEAD : base + (j + 1) * HEAD] = v.astype(BF16)
        end = base + (group + 1) * HEAD
        packed[:, end : end + HEAD] = y[:, end : end + HEAD].astype(BF16)


def qkv_call(t, xs, ws, gains, packed_gains, cos, sin, width, kv_heads, group):
    rows = xs[0].shape[0]
    n = rows * len(xs)
    cols = kv_heads * (group + 2) * HEAD
    kept = kv_heads * (group + 1) * HEAD
    return call(
        functools.partial(qkv_kernel, len(xs), len(ws), packed_gains, kv_heads, group),
        (len(xs),),
        [part_at((rows, width), 0) for _ in xs]
        + [part_at((w.shape[0], cols), 0) for w in ws]
        + [whole(gains.shape), rows_xor(rows, HEAD), rows_xor(rows, HEAD)],
        [rows_at(rows, width), rows_xor(rows, cols), rows_xor(rows, kept), whole((8, width))],
        [
            shape_of((n, width)),
            shape_of((n, cols)),
            shape_of((n, kept), F32),
            shape_of((8, width), F32),
        ],
        2 * n * width * cols,
        [pltpu.VMEM((width, cols), BF16), pltpu.VMEM((rows, width), BF16)],
    )(t, *xs, *ws, gains, cos, sin)


def weights_of(q, k, same, causal):
    e = jnp.exp2(mm(k, q, 1, 1) * EXP2_SCALE)
    keep = same if causal is None else same & causal
    return jnp.where(keep, e, 0.0)


def accumulate(part, acc):
    h = pl.program_id(0)

    @pl.when(h == 0)
    def _():
        acc[...] = part

    @pl.when(h > 0)
    def _():
        acc[...] += part


def split_rows(rows, acc, keep, send):
    for k in range(acc.shape[0] // rows):
        out = send if k % 2 else keep
        at = (k // 2) * rows
        out[at : at + rows, :] = acc[k * rows : (k + 1) * rows, :].astype(BF16)


def attn_forward_kernel(rows, blocks, group, kv_heads, nw, t, packed, seg_col, seg_row, *refs):
    ws = refs[:nw]
    mixed, inv, keep, send, w, acc = refs[nw:]
    causal = lax.broadcasted_iota(jnp.int32, (rows, rows), 0) <= lax.broadcasted_iota(
        jnp.int32, (rows, rows), 1
    )
    kc = group * HEAD
    join(ws, w)
    for i in range(blocks):
        lo = i * rows
        at = pl.multiple_of(lax.bitwise_xor(i, t[0]) * rows, rows)
        sq = seg_row[:, lo : lo + rows]
        for j in range(group):
            q = packed[lo : lo + rows, j * HEAD : (j + 1) * HEAD]
            parts = []
            total = jnp.zeros((1, rows), F32)
            for b in range(i + 1):
                k = packed[b * rows : (b + 1) * rows, kc : kc + HEAD]
                same = seg_col[b * rows : (b + 1) * rows, :] == sq
                e = weights_of(q, k, same, causal if b == i else None)
                total = total + jnp.sum(e, axis=0, keepdims=True)
                parts.append(e)
            rec = 1.0 / total
            inv[0, j : j + 1, lo : lo + rows] = rec
            out = jnp.zeros((rows, HEAD), F32)
            for b in range(i + 1):
                v = packed[b * rows : (b + 1) * rows, kc + HEAD : kc + 2 * HEAD]
                out = out + mm((parts[b] * rec).astype(BF16), v, 0, 0)
            mixed[pl.ds(at, rows), j * HEAD : (j + 1) * HEAD] = out.astype(BF16)
    accumulate(mm(mixed[...], w[...], 1, 1), acc)

    @pl.when(pl.program_id(0) == kv_heads - 1)
    def _():
        split_rows(rows, acc, keep, send)


def by_head(n, width, first=0):
    return pl.BlockSpec((n, width), lambda h, t: (0, first + h))


def attn_forward(t, packed, seg_col, seg_row, w_o, first, rows, width, kv_heads, group):
    n = packed.shape[0]
    q_cols = group * HEAD
    return call(
        functools.partial(attn_forward_kernel, rows, n // rows, group, kv_heads, len(w_o)),
        (kv_heads,),
        [by_head(n, q_cols + 2 * HEAD), whole(seg_col.shape), whole(seg_row.shape)]
        + [by_head(w.shape[0], q_cols, first) for w in w_o],
        [
            by_head(n, q_cols),
            pl.BlockSpec((1, 8, n), lambda h, t: (h, 0, 0)),
            whole((n // 2, width)),
            whole((n // 2, width)),
        ],
        [
            shape_of((n, kv_heads * q_cols)),
            shape_of((kv_heads, 8, n), F32),
            shape_of((n // 2, width)),
            shape_of((n // 2, width)),
        ],
        kv_heads * group * n * n * HEAD * 4,
        [pltpu.VMEM((width, q_cols), BF16), pltpu.VMEM((n, width), F32)],
    )(t, packed, seg_col, seg_row, *w_o)


def head_back(e, u, cos, sin, gain):
    e = e * cos - pltpu.roll(e, HEAD // 2, 1) * sin
    r = lax.rsqrt(jnp.mean(u * u, axis=1, keepdims=True) + EPS)
    ur = u * r
    dgain = jnp.sum(e * ur, axis=0, keepdims=True)
    ec = e * gain
    du = r * (ec - ur * jnp.mean(ur * ec, axis=1, keepdims=True))
    return du, dgain


def fill_gain_rows(d_attn, d_mlp, d_heads, outs):
    n = outs[0].shape[0] // GAIN_ROWS
    at = lax.broadcasted_iota(jnp.int32, (GAIN_ROWS, 4 * HEAD), 0)
    for k, out in enumerate(outs):
        out[...] = jnp.zeros_like(out)
        for p in range(n):
            here = slice((k * n + p) * HEAD, (k * n + p + 1) * HEAD)
            row = jnp.concatenate(
                [d_attn[0:1, here], d_mlp[0:1, here], d_heads[0:1], d_heads[1:2]], axis=1
            )
            rows = slice(p * GAIN_ROWS, (p + 1) * GAIN_ROWS)
            out[rows, : 4 * HEAD] = jnp.where(at == 0, row, 0.0).astype(BF16)


def attn_backward_kernel(rows, blocks, group, kv_heads, nw, packed_gains, t, *refs):
    packed, seg_col, seg_row, inv, raw, cos, sin, gains, dgain_mlp = refs[:9]
    refs = refs[9:]
    branch, refs = refs[:blocks], refs[blocks:]
    xs, refs = refs[:blocks], refs[blocks:]
    w_os, refs = refs[:nw], refs[nw:]
    w_qkvs, refs = refs[:nw], refs[nw:]
    dpacked, dgain, keep, send, dgain_x, *tails, dk, dv, dmix, w_o, w_qkv, acc, heads = refs
    causal = lax.broadcasted_iota(jnp.int32, (rows, rows), 0) <= lax.broadcasted_iota(
        jnp.int32, (rows, rows), 1
    )
    kc = group * HEAD
    gq = gains[2:3, :HEAD]
    gk = gains[3:4, :HEAD]
    join(w_os, w_o)
    join(w_qkvs, w_qkv)
    for k in range(blocks):
        dmix[k * rows : (k + 1) * rows, :] = mm(branch[k][...], w_o[...]).astype(BF16)
    dk[...] = jnp.zeros_like(dk)
    dv[...] = jnp.zeros_like(dv)
    dgain[...] = jnp.zeros_like(dgain)
    for i in range(blocks):
        lo = i * rows
        at = pl.multiple_of(lax.bitwise_xor(i, t[0]) * rows, rows)
        sq = seg_row[:, lo : lo + rows]
        for j in range(group):
            q = packed[lo : lo + rows, j * HEAD : (j + 1) * HEAD]
            do = dmix[pl.ds(at, rows), j * HEAD : (j + 1) * HEAD]
            rec = inv[0, j : j + 1, lo : lo + rows]
            probs = []
            dprobs = []
            delta = jnp.zeros((1, rows), F32)
            for b in range(i + 1):
                here = slice(b * rows, (b + 1) * rows)
                k = packed[here, kc : kc + HEAD]
                v = packed[here, kc + HEAD : kc + 2 * HEAD]
                same = seg_col[here, :] == sq
                p = weights_of(q, k, same, causal if b == i else None) * rec
                dp = mm(v, do, 1, 1)
                delta = delta + jnp.sum(p * dp, axis=0, keepdims=True)
                dv[here, :] += mm(p.astype(BF16), do)
                probs.append(p)
                dprobs.append(dp)
            dq = jnp.zeros((rows, HEAD), F32)
            for b in range(i + 1):
                here = slice(b * rows, (b + 1) * rows)
                k = packed[here, kc : kc + HEAD]
                ds = (probs[b] * (dprobs[b] - delta)).astype(BF16)
                dk[here, :] += mm(ds, q)
                dq = dq + mm(ds, k, 0, 0)
            du, dg = head_back(
                dq * SCALE,
                raw[lo : lo + rows, j * HEAD : (j + 1) * HEAD],
                cos[lo : lo + rows, :],
                sin[lo : lo + rows, :],
                gq,
            )
            dgain[0, 0:1, :] += dg
            dpacked[pl.ds(at, rows), j * HEAD : (j + 1) * HEAD] = du.astype(BF16)
    for i in range(blocks):
        here = slice(i * rows, (i + 1) * rows)
        at = pl.multiple_of(lax.bitwise_xor(i, t[0]) * rows, rows)
        du, dg = head_back(
            dk[here, :] * SCALE, raw[here, kc : kc + HEAD], cos[here, :], sin[here, :], gk
        )
        dgain[0, 1:2, :] += dg
        dpacked[pl.ds(at, rows), kc : kc + HEAD] = du.astype(BF16)
        dpacked[pl.ds(at, rows), kc + HEAD : kc + 2 * HEAD] = dv[here, :].astype(BF16)
    accumulate(mm(dpacked[...], w_qkv[...], 1, 1), acc)
    accumulate(dgain[0], heads)

    @pl.when(pl.program_id(0) == kv_heads - 1)
    def _():
        total = jnp.zeros((1, acc.shape[1]), F32)
        for k in range(blocks):
            u = xs[k][...].astype(F32)
            ur = u * lax.rsqrt(jnp.mean(u * u, axis=1, keepdims=True) + EPS)
            total = total + jnp.sum(acc[k * rows : (k + 1) * rows, :] * ur, axis=0, keepdims=True)
        dgain_x[...] = jnp.broadcast_to(total, dgain_x.shape)
        if packed_gains:
            fill_gain_rows(dgain_x, dgain_mlp, heads[...], tails)
        split_rows(rows, acc, keep, send)


def attn_backward(
    t,
    packed_gains,
    packed,
    seg_col,
    seg_row,
    inv,
    raw,
    cos,
    sin,
    gains,
    dgain_mlp,
    branch,
    xs,
    w_o,
    first,
    w_qkv,
    width,
    kv_heads,
    group,
):
    n = packed.shape[0]
    rows = xs[0].shape[0]
    q_cols = group * HEAD
    cols = q_cols + 2 * HEAD
    tails = [(len(w_o) // 2 * GAIN_ROWS, kv_heads * cols)] * 2 if packed_gains else []
    return call(
        functools.partial(
            attn_backward_kernel, rows, n // rows, group, kv_heads, len(w_o), packed_gains
        ),
        (kv_heads,),
        [
            by_head(n, cols),
            whole(seg_col.shape),
            whole(seg_row.shape),
            pl.BlockSpec((1, 8, n), lambda h, t: (h, 0, 0)),
            by_head(n, q_cols + HEAD),
            whole(cos.shape),
            whole(sin.shape),
            whole(gains.shape),
            whole(dgain_mlp.shape),
        ]
        + [whole(b.shape) for b in branch]
        + [part_at((rows, width), 0) for _ in xs]
        + [by_head(w.shape[0], q_cols, first) for w in w_o]
        + [by_head(w.shape[0], cols) for w in w_qkv],
        [
            by_head(n, cols),
            pl.BlockSpec((1, 8, HEAD), lambda h, t: (h, 0, 0)),
            whole((n // 2, width)),
            whole((n // 2, width)),
            whole((8, width)),
        ]
        + [whole(shape) for shape in tails],
        [
            shape_of(packed.shape),
            shape_of((kv_heads, 8, HEAD), F32),
            shape_of((n // 2, width)),
            shape_of((n // 2, width)),
            shape_of((8, width), F32),
        ]
        + [shape_of(shape) for shape in tails],
        kv_heads * group * n * n * HEAD * 10,
        [
            pltpu.VMEM((n, HEAD), F32),
            pltpu.VMEM((n, HEAD), F32),
            pltpu.VMEM((n, q_cols), BF16),
            pltpu.VMEM((width, q_cols), BF16),
            pltpu.VMEM((width, cols), BF16),
            pltpu.VMEM((n, width), F32),
            pltpu.VMEM((8, HEAD), F32),
        ],
    )(t, packed, seg_col, seg_row, inv, raw, cos, sin, gains, dgain_mlp, *branch, *xs, *w_o, *w_qkv)


def join_in_order(t, reorder, block, out):
    if not reorder:
        out[...] = block[...]
        return
    for p in range(out.shape[0] // HEAD):
        out[p * HEAD : (p + 1) * HEAD, :] = block[pl.ds(model_block(t, p), HEAD), :]


def mlp_kernel(ff, nx, reorder, t, *refs):
    xs, refs = refs[:nx], refs[nx:]
    gs, refs = refs[:nx], refs[nx:]
    w_gu, w_d, *refs = refs
    act, dgu, x_out, g_out, dx_keep, dx_send, out_keep, out_send, w, wd, x, g = refs
    i = pl.program_id(0)

    @pl.when(i == 0)
    def _():
        join_in_order(t, reorder, w_gu, w)
        join_in_order(t, reorder, w_d, wd)

    for k in range(nx):

        @pl.when(i == k)
        def _(k=k):
            x[...] = xs[k][...]
            g[...] = gs[k][...]
            store_columns(t, reorder, xs[k][...], x_out)
            g_out[...] = gs[k][...]

    y = mm(x[...], w[...])
    gate = y[:, :ff]
    up = y[:, ff:]
    sig = 1.0 / (1.0 + jnp.exp(-gate))
    silu = gate * sig
    a = (silu * up).astype(BF16)
    act[...] = a
    da = mm(g[...], wd[...])
    dgu[:, :ff] = (da * up * sig * (1.0 + gate * (1.0 - sig))).astype(BF16)
    dgu[:, ff:] = (da * silu).astype(BF16)
    dx = mm(dgu[...], w[...], 1, 1).astype(BF16)
    out = mm(a, wd[...], 1, 1).astype(BF16)

    @pl.when(lax.rem(i, 2) == 0)
    def _():
        dx_keep[...] = dx
        out_keep[...] = out

    @pl.when(lax.rem(i, 2) == 1)
    def _():
        dx_send[...] = dx
        out_send[...] = out


def mlp_call(t, reorder, xs, gs, g_index, w_gu, w_d, d_index, ff, width):
    rows = xs[0].shape[0]
    n = rows * len(xs)
    halves = pl.BlockSpec((rows, width), lambda i, t: (lax.div(i, 2), 0))
    return call(
        functools.partial(mlp_kernel, ff, len(xs), reorder),
        (len(xs),),
        [whole(x.shape) for x in xs]
        + [part_at((rows, width), g_index) for _ in gs]
        + [part_at((width, 2 * ff), 0), part_at((width, ff), d_index)],
        [rows_at(rows, ff), rows_at(rows, 2 * ff)] + [rows_at(rows, width)] * 2 + [halves] * 4,
        [shape_of((n, ff)), shape_of((n, 2 * ff))]
        + [shape_of((n, width))] * 2
        + [shape_of((n // 2, width))] * 4,
        2 * n * width * ff * 6,
        [
            pltpu.VMEM((width, 2 * ff), BF16),
            pltpu.VMEM((width, ff), BF16),
            pltpu.VMEM((rows, width), BF16),
            pltpu.VMEM((rows, width), BF16),
        ],
    )(t, *xs, *gs, w_gu, w_d)


def sum_of(parts):
    total = parts[0][...].astype(F32)
    for p in parts[1:]:
        total = total + p[...].astype(F32)
    return total


def hidden_kernel(n_parts, t, *refs):
    parts = refs[:n_parts]
    x, gains, hidden, normed = refs[n_parts:]
    h = x[...].astype(F32) + sum_of(parts)
    hidden[...] = h
    r = lax.rsqrt(jnp.mean(h * h, axis=1, keepdims=True) + EPS)
    normed[...] = (h * r * gains[1:2, :]).astype(BF16)


def row_tile(rows, width, index=0):
    return pl.BlockSpec((rows // ROW_STEPS, width), lambda i, t: (i, index))


def hidden_call(t, parts, x, gains, rows, width):
    spec = row_tile(rows, width)
    return call(
        functools.partial(hidden_kernel, len(parts)),
        (ROW_STEPS,),
        [spec for _ in parts] + [spec, whole(gains.shape)],
        [spec, spec],
        [shape_of((rows, width), F32), shape_of((rows, width))],
        rows * width * 8,
    )(t, *parts, x, gains)


def norm_back(e, u, gain):
    r = lax.rsqrt(jnp.mean(u * u, axis=1, keepdims=True) + EPS)
    ur = u * r
    ec = e * gain
    return r * (ec - ur * jnp.mean(ur * ec, axis=1, keepdims=True)), jnp.sum(e * ur, axis=0, keepdims=True)


def d_hidden_kernel(n_parts, t, *refs):
    parts = refs[:n_parts]
    hidden, g, gains, d_hidden, branch, d_gain = refs[n_parts:]
    du, dg = norm_back(sum_of(parts), hidden[...], gains[1:2, :])
    d = g[...].astype(F32) + du
    d_hidden[...] = d
    branch[...] = d.astype(BF16)
    accumulate(jnp.broadcast_to(dg, d_gain.shape), d_gain)


def d_hidden_call(t, parts, hidden, g, g_index, gains, rows, width):
    spec = row_tile(rows, width)
    return call(
        functools.partial(d_hidden_kernel, len(parts)),
        (ROW_STEPS,),
        [spec for _ in parts] + [spec, row_tile(rows, width, g_index), whole(gains.shape)],
        [spec, spec, whole((8, width))],
        [shape_of((rows, width), F32), shape_of((rows, width)), shape_of((8, width), F32)],
        rows * width * 12,
    )(t, *parts, hidden, g, gains)


def store_columns(t, reorder, value, out):
    if not reorder:
        out[...] = value
        return
    for p in range(value.shape[1] // HEAD):
        out[:, pl.ds(model_block(t, p), HEAD)] = value[:, p * HEAD : (p + 1) * HEAD]


def activations_kernel(n_parts, reorder, t, *refs):
    parts = refs[:n_parts]
    hidden, out = refs[n_parts:]
    store_columns(t, reorder, (hidden[...] + sum_of(parts)).astype(BF16), out)


def activations_call(t, reorder, parts, hidden, rows, width):
    spec = row_tile(rows, width)
    return call(
        functools.partial(activations_kernel, len(parts), reorder),
        (ROW_STEPS,),
        [spec for _ in parts] + [spec],
        spec,
        shape_of((rows, width)),
        rows * width * 2,
    )(t, *parts, hidden)


def d_tokens_kernel(n_parts, reorder, t, *refs):
    parts = refs[:n_parts]
    x, d_hidden, gains, out = refs[n_parts:]
    du, _ = norm_back(sum_of(parts), x[...].astype(F32), gains[0:1, :])
    store_columns(t, reorder, d_hidden[...] + du, out)


def d_tokens_call(t, reorder, parts, x, d_hidden, gains, rows, width):
    spec = row_tile(rows, width)
    return call(
        functools.partial(d_tokens_kernel, len(parts), reorder),
        (ROW_STEPS,),
        [spec for _ in parts] + [spec, spec, whole(gains.shape)],
        spec,
        shape_of((rows, width), F32),
        rows * width * 12,
    )(t, *parts, x, d_hidden, gains)


def outer_half(left, right, half):
    m = left.shape[1] // 2
    return mm(left[:, half * m : (half + 1) * m], right, 0, 0).astype(BF16)


def shard_of(parts):
    total = parts[0].astype(F32)
    for p in parts[1:]:
        total = total + p.astype(F32)
    return total


def unpack_heads(kv_heads, group, w):
    q, k, v = [], [], []
    for h in range(kv_heads):
        base = h * (group + 2) * HEAD
        mid = base + group * HEAD
        q.append(w[:, base:mid])
        k.append(w[:, mid : mid + HEAD])
        v.append(w[:, mid + HEAD : mid + 2 * HEAD])
    join = lambda parts: jnp.concatenate(parts, axis=1)
    return join(q), join(k), join(v)


def pair_sum_kernel(t, keep, rows, got, *outs):
    n = keep.shape[0] // len(outs)
    for z, out in enumerate(outs):
        here = slice(z * n, (z + 1) * n)
        low = slice(z * GAIN_ROWS, (z + 1) * GAIN_ROWS)
        there = slice(keep.shape[0] + z * GAIN_ROWS, keep.shape[0] + (z + 1) * GAIN_ROWS)
        out[:n, :] = (keep[here, :].astype(F32) + got[here, :].astype(F32)).astype(out.dtype)
        out[n:, :] = (rows[low, :].astype(F32) + got[there, :].astype(F32)).astype(out.dtype)


def pair_sum(t, keep, rows, got, parts):
    m, cols = keep.shape
    n = m // parts + GAIN_ROWS
    return call(
        pair_sum_kernel,
        (1,),
        [whole(keep.shape), whole(rows.shape), whole(got.shape)],
        [whole((n, cols)) for _ in range(parts)],
        [shape_of((n, cols), F32 if z == 0 else BF16) for z in range(parts)],
        m * cols,
    )(t, keep, rows, got)


def xor_pairs(size, bits):
    return [(i, i ^ bits) for i in range(size)]


class Links:
    def __init__(self, dp, tensor):
        self.dp, self.tensor = dp, tensor
        self.direct = (dp, tensor) == (8, 4)
        self.d = lax.axis_index("dp")
        self.t = lax.axis_index("tensor")

    def over_dp(self, x, bits):
        return lax.ppermute(x, "dp", xor_pairs(self.dp, bits))

    def over_tensor(self, x, bits):
        return lax.ppermute(x, "tensor", xor_pairs(self.tensor, bits))

    def offsets(self):
        if self.direct:
            return jnp.stack([self.t, self.d])
        return jnp.zeros((2,), jnp.int32)

    def gather_dp(self, x):
        if not self.direct:
            return [lax.all_gather(x, "dp", axis=0, tiled=True)]
        own = self.gather_z(x)
        return own + [self.over_dp(b, 1) for b in own]

    def gather_z(self, x):
        return [x] + [self.over_dp(x, 2 * z) for z in (1, 2, 3)]

    def send_half(self, left, right):
        send = outer_half(left, right, 1)
        if self.direct:
            send = self.over_dp(send, 1)
        return send, outer_half(left, right, 0)

    def send_quarters(self, got, keep):
        if not self.direct:
            both = jnp.concatenate([keep, got], axis=0)
            return [lax.psum_scatter(both, "dp", scatter_dimension=0, tiled=True)]
        n = keep.shape[0] // 4
        part = lambda z: keep[z * n : (z + 1) * n].astype(F32) + got[z * n : (z + 1) * n].astype(F32)
        return [part(0)] + [self.over_dp(part(z).astype(BF16), 2 * z) for z in (1, 2, 3)]

    def gather_tensor(self, x, *after):
        if not self.direct:
            full = lax.all_gather(x, "tensor", axis=0, tiled=True)
            return jnp.split(full, self.tensor, axis=0)
        far = self.over_tensor(x, 2)
        return [x, self.over_tensor(x, 1), far, self.over_tensor(tie(far, *after) if after else far, 1)]

    def scatter_tensor(self, keep, send, sent=False):
        rows = 2 * keep.shape[0] // self.tensor
        if not self.direct:
            blocks = []
            for k in range(self.tensor // 2):
                blocks += [keep[k * rows : (k + 1) * rows], send[k * rows : (k + 1) * rows]]
            full = jnp.concatenate(blocks, axis=0)
            return [lax.psum_scatter(full, "tensor", scatter_dimension=0, tiled=True)]
        got = send if sent else self.over_tensor(send, 1)
        far = keep[rows:].astype(F32) + got[rows:].astype(F32)
        far = far.astype(BF16)
        return [keep, got, self.over_tensor(far, 2), far]


def rope_tables(offsets):
    frequency = ROPE_BASE ** (-(2.0 * jnp.arange(HEAD // 2, dtype=F32)) / HEAD)
    angles = offsets.astype(F32)[:, None] * frequency[None, :]
    cos, sin = jnp.cos(angles), jnp.sin(angles)
    return jnp.concatenate([cos, cos], axis=1), jnp.concatenate([-sin, sin], axis=1)


def pack_heads(wq, wk, wv, group):
    parts = []
    for h in range(wk.shape[1] // HEAD):
        parts += [
            wq[:, h * group * HEAD : (h + 1) * group * HEAD],
            wk[:, h * HEAD : (h + 1) * HEAD],
            wv[:, h * HEAD : (h + 1) * HEAD],
        ]
    return jnp.concatenate(parts, axis=1)


def body(
    dp,
    tensor,
    tokens,
    segment_ids,
    positions,
    w_query,
    key_projection,
    value_projection,
    w_out,
    w_gate,
    w_up,
    w_down,
    gain_attn,
    gain_mlp,
    gain_query,
    gain_key,
    cotangent,
):
    links = Links(dp, tensor)
    direct = links.direct
    rows, width = tokens.shape
    kv_heads = key_projection.shape[1] // HEAD
    group = w_query.shape[1] // key_projection.shape[1]
    q_cols = group * HEAD
    ff = w_gate.shape[1]
    head_part = HEAD // dp
    t = links.offsets()

    if direct:
        w_attn = pack_attn(
            t,
            w_query,
            key_projection,
            value_projection,
            w_out,
            (gain_attn, gain_mlp, gain_query, gain_key),
            kv_heads,
            group,
        )
        both = pack_rows(t, tie(tokens, w_attn), cotangent)
        w_mlp = pack_mlp(t, tie(w_gate, both), w_up, w_down)
        attn_near = links.gather_z(w_attn)
        attn_far = links.over_dp(w_attn, 1)
        beside = links.over_tensor(both, 1)
        far = links.over_tensor(both, 2)
        across = tie(far, attn_far, attn_near[1], attn_near[2])
        rows_all = [both, beside, far, links.over_tensor(across, 1)]
        w_attn = attn_near + [attn_far] + [links.over_dp(b, 1) for b in attn_near[1:]]
        w_mlp = tie(w_mlp, (far, attn_far, attn_near[1], attn_near[2], w_attn[5]))
        w_qkv, w_o, o_index = w_attn, w_attn, kv_heads * (group + 2) * HEAD // q_cols
        w_gu = w_d = lax.all_gather(w_mlp, "dp", axis=0, tiled=True)
        d_index = 2
        gains = jnp.zeros((8, width), F32)
    else:
        w_qkv = links.gather_dp(pack_heads(w_query, key_projection, value_projection, group))
        w_o = links.gather_dp(w_out.T)
        w_gu = links.gather_dp(jnp.concatenate([w_gate, w_up], axis=1))[0]
        w_d = links.gather_dp(w_down.T)[0]
        d_index, o_index = 0, 0
        row = lambda g: jnp.pad(g, (0, width - g.shape[0]))[None, :].astype(F32)
        whole_gain = lambda g: row(lax.all_gather(g, "dp", axis=0, tiled=True))
        gains = jnp.concatenate(
            [whole_gain(g) for g in (gain_attn, gain_mlp, gain_query, gain_key)]
            + [jnp.zeros((4, width), F32)],
            axis=0,
        )
        rows_all = links.gather_tensor(jnp.concatenate([tokens, cotangent], axis=1))
    own = rows_all[0] if direct else jnp.concatenate([tokens, cotangent], axis=1)

    cos, sin = rope_tables(positions[0])
    seg_row = segment_ids
    seg_col = segment_ids.reshape(-1, 1)

    normed, packed, raw, gains = qkv_call(
        t, rows_all, w_qkv, gains, direct, cos, sin, width, kv_heads, group
    )
    mixed, inv, keep, send = attn_forward(
        t, packed, seg_col, seg_row, w_o, o_index, rows, width, kv_heads, group
    )
    parts = links.scatter_tensor(keep, send)
    hidden, normed_mlp = hidden_call(t, parts[:3], own, gains, rows, width)
    normed_mlp = links.gather_tensor(normed_mlp)
    act, d_gu, normed_mlp, cot, dx_keep, dx_send, out_keep, out_send = mlp_call(
        t, direct, normed_mlp, rows_all, 1, w_gu, w_d, d_index, ff, width
    )
    parts = links.scatter_tensor(dx_keep, dx_send)
    down = links.send_half(cot, tie(act, parts[1:2]))
    d_hidden, branch, d_gain_mlp = d_hidden_call(t, parts[:3], hidden, own, 1, gains, rows, width)
    gu_sum = mm(normed_mlp, tie(d_gu, branch), 0, 0).astype(BF16)
    gu = lax.psum_scatter(gu_sum, "dp", scatter_dimension=0, tiled=True)
    branch = links.gather_tensor(branch, gu_sum, down[0])
    down = links.send_quarters(*down)
    out_parts = links.scatter_tensor(out_keep, tie(out_send, branch))[:3]
    branch_rows = jnp.concatenate(branch, axis=0)
    out_sent = outer_half(branch_rows, mixed, 1)
    if direct:
        out_sent = links.over_dp(out_sent, 1)
    d_packed, d_gain_heads, keep, send, d_gain_attn, *tails = tie(
        attn_backward(
            t, direct, packed, seg_col, seg_row, inv, raw, cos, sin, gains, d_gain_mlp, branch, rows_all,
            w_o, o_index, w_qkv, width, kv_heads, group,
        ),
        out_sent,
        down[1:],
        out_parts,
    )
    if direct:
        send_qkv = jnp.concatenate([outer_half(normed, d_packed, 1), tails[1]], axis=0)
        got = links.over_dp(send_qkv, 1)
    parts = links.scatter_tensor(keep, send)[:3]
    out = (out_sent, outer_half(branch_rows, tie(mixed, parts[:2]), 0))
    out = links.send_quarters(*tie(out, parts[:2]))
    if direct:
        keep_qkv = outer_half(normed, d_packed, 0)
        qkv = pair_sum(t, keep_qkv, tails[0], tie(got, out[1:], parts[2]), 4)
        qkv = [qkv[0]] + [links.over_dp(qkv[z], 2 * z) for z in (1, 2, 3)]
    else:
        qkv = links.send_quarters(*links.send_half(normed, d_packed))
    d_tokens = d_tokens_call(t, direct, parts, own, d_hidden, gains, rows, width)
    activations = activations_call(t, direct, out_parts, hidden, rows, width)
    grad_down = shard_of(down).T
    grad_gate, grad_up = gu[:, :ff].astype(F32), gu[:, ff:].astype(F32)
    grad_out = shard_of(out).T
    n = width // dp
    qkv = shard_of(qkv)
    grad_query, grad_key, grad_value = unpack_heads(kv_heads, group, qkv[:n])
    if direct:
        sums = qkv[n : n + 1, : 4 * HEAD]
        sums = sums + links.over_tensor(sums, 1)
        sums = (sums + links.over_tensor(sums, 2)).reshape(4, HEAD)
        sum_attn, sum_mlp, sum_query, sum_key = sums[0], sums[1], sums[2], sums[3]
    else:
        heads = jnp.sum(d_gain_heads, axis=0)
        sum_attn, sum_mlp, sum_query, sum_key = lax.psum(
            (d_gain_attn[0], d_gain_mlp[0], heads[0], heads[1]), ("dp", "tensor")
        )
        sum_attn = lax.dynamic_slice_in_dim(sum_attn, links.d * n, n, 0)
        sum_mlp = lax.dynamic_slice_in_dim(sum_mlp, links.d * n, n, 0)
    shard = lambda v: lax.dynamic_slice_in_dim(v, links.d * head_part, head_part, 0)
    return (
        activations,
        d_tokens,
        grad_query,
        grad_key,
        grad_value,
        grad_out,
        grad_gate,
        grad_up,
        grad_down,
        sum_attn,
        sum_mlp,
        shard(sum_query),
        shard(sum_key),
    )


def solution(mesh):
    tokens = P(("dp", "tensor"), None)
    by_rows = P("dp", "tensor")
    by_columns = P("tensor", "dp")
    sequence = P("dp", None)
    gain = P("dp")
    return jax.shard_map(
        functools.partial(body, mesh.shape["dp"], mesh.shape["tensor"]),
        mesh=mesh,
        in_specs=(
            tokens,
            sequence,
            sequence,
            by_rows,
            by_rows,
            by_rows,
            by_columns,
            by_rows,
            by_rows,
            by_columns,
            gain,
            gain,
            gain,
            gain,
            tokens,
        ),
        out_specs=(
            tokens,
            tokens,
            by_rows,
            by_rows,
            by_rows,
            by_columns,
            by_rows,
            by_rows,
            by_columns,
            gain,
            gain,
            gain,
            gain,
        ),
        check_vma=False,
    )
```

```python
import functools

import jax
import jax.numpy as jnp
from jax import lax
from jax.experimental import pallas as pl
from jax.experimental.pallas import tpu as pltpu
from jax.sharding import PartitionSpec as P

HEAD = 128
EPS = 1e-06
ROPE_BASE = 1000000.0
SCALE = HEAD ** (-0.5)
EXP2_SCALE = SCALE * 1.4426950408889634
F32 = jnp.float32
BF16 = jnp.bfloat16
VMEM_LIMIT = 60 * 1024 * 1024
ORDER = (0, 2, 4, 6, 1, 3, 5, 7)
GAIN_ROWS = 16
ROW_STEPS = 1


def mm(a, b, ca=1, cb=0):
    return lax.dot_general(a, b, (((ca,), (cb,)), ((), ())), preferred_element_type=F32)


def shape_of(shape, dtype=BF16):
    return jax.ShapeDtypeStruct(shape, dtype)


def call(kernel, grid, in_specs, out_specs, out_shape, flops, scratch=()):
    return pl.pallas_call(
        kernel,
        out_shape=out_shape,
        grid_spec=pltpu.PrefetchScalarGridSpec(
            num_scalar_prefetch=1,
            grid=grid,
            in_specs=in_specs,
            out_specs=out_specs,
            scratch_shapes=list(scratch),
        ),
        compiler_params=pltpu.CompilerParams(
            dimension_semantics=("arbitrary",) * len(grid), vmem_limit_bytes=VMEM_LIMIT
        ),
        cost_estimate=pl.CostEstimate(flops=1, bytes_accessed=1, transcendentals=0),
    )


def tie(x, *after):
    return lax.optimization_barrier((x, after))[0]


def whole(shape):
    return pl.BlockSpec(shape, lambda i, t: (0,) * len(shape))


def part_at(shape, index):
    return pl.BlockSpec(shape, lambda i, t: (0, index))


def rows_at(rows, cols):
    return pl.BlockSpec((rows, cols), lambda i, t: (i, 0))


def rows_xor(rows, cols):
    return pl.BlockSpec((rows, cols), lambda i, t: (lax.bitwise_xor(i, t[0]), 0))


def model_block(t, p):
    return pl.multiple_of(lax.bitwise_xor(t[1], ORDER[p]) * HEAD, HEAD)


def pack_attn_kernel(kv_heads, group, t, wq, wk, wv, wo, g_attn, g_mlp, g_query, g_key, out):
    n = wq.shape[0]
    for h in range(kv_heads):
        base = h * (group + 2) * HEAD
        mid = base + group * HEAD
        out[:n, base:mid] = wq[:, h * group * HEAD : (h + 1) * group * HEAD]
        out[:n, mid : mid + HEAD] = wk[:, h * HEAD : (h + 1) * HEAD]
        out[:n, mid + HEAD : mid + 2 * HEAD] = wv[:, h * HEAD : (h + 1) * HEAD]
    out[:n, kv_heads * (group + 2) * HEAD :] = wo[...].T
    out[n:, :] = jnp.zeros((GAIN_ROWS, out.shape[1]), BF16)
    m = g_query.shape[1]
    place = lax.broadcasted_iota(jnp.int32, (m, HEAD), 0) + t[1] * m == lax.broadcasted_iota(
        jnp.int32, (m, HEAD), 1
    )
    place = jnp.where(place, 1.0, 0.0).astype(BF16)
    rows = (g_attn[...].astype(F32), g_mlp[...].astype(F32), mm(g_query[...], place), mm(g_key[...], place))
    at = lax.broadcasted_iota(jnp.int32, (GAIN_ROWS, HEAD), 0)
    tile = jnp.zeros((GAIN_ROWS, HEAD), F32)
    for k, row in enumerate(rows):
        tile = jnp.where(at == k, row, tile)
    out[n:, :HEAD] = tile.astype(BF16)


def pack_attn(t, wq, wk, wv, wo, gains, kv_heads, group):
    n = wq.shape[0]
    cols = kv_heads * (group + 2) * HEAD + wo.shape[0]
    args = (wq, wk, wv, wo, *[g[None, :] for g in gains])
    return call(
        functools.partial(pack_attn_kernel, kv_heads, group),
        (1,),
        [whole(a.shape) for a in args],
        whole((n + GAIN_ROWS, cols)),
        shape_of((n + GAIN_ROWS, cols)),
        n * cols,
    )(t, *args)


def pack_rows_kernel(t, x, g, out):
    width = x.shape[1]
    for p in range(width // HEAD):
        at = model_block(t, p)
        out[:, p * HEAD : (p + 1) * HEAD] = x[:, pl.ds(at, HEAD)]
        out[:, width + p * HEAD : width + (p + 1) * HEAD] = g[:, pl.ds(at, HEAD)]


def pack_rows(t, x, g):
    n, width = x.shape
    return call(
        pack_rows_kernel,
        (1,),
        [whole(x.shape), whole(g.shape)],
        whole((n, 2 * width)),
        shape_of((n, 2 * width)),
        n * width,
    )(t, x, g)


def pack_mlp_kernel(t, wg, wu, wd, out):
    ff = wg.shape[1]
    out[:, :ff] = wg[...]
    out[:, ff : 2 * ff] = wu[...]
    out[:, 2 * ff :] = wd[...].T


def pack_mlp(t, wg, wu, wd):
    shape = (wg.shape[0], 3 * wg.shape[1])
    args = (wg, wu, wd)
    return call(
        pack_mlp_kernel,
        (1,),
        [whole(a.shape) for a in args],
        whole(shape),
        shape_of(shape),
        shape[0] * shape[1],
    )(t, *args)


def join(blocks, out):
    n = out.shape[0] // len(blocks)
    for p, b in enumerate(blocks):
        out[p * n : (p + 1) * n, :] = b[:n, :]


def qkv_kernel(nx, nw, packed_gains, kv_heads, group, t, *refs):
    xs, ws = refs[:nx], refs[nx : nx + nw]
    gains_in, cos, sin, normed, packed, raw, gains, w, x = refs[nx + nw :]
    i = pl.program_id(0)

    @pl.when(i == 0)
    def _():
        join(ws, w)
        if packed_gains:
            n = w.shape[0] // nw
            gains[...] = jnp.zeros_like(gains)
            heads = jnp.zeros((GAIN_ROWS, HEAD), F32)
            for p, b in enumerate(ws):
                tile = b[n:, :HEAD].astype(F32)
                gains[0:2, p * n : (p + 1) * n] = tile[0:2]
                heads = heads + tile
            gains[2:4, :HEAD] = heads[2:4]
        else:
            gains[...] = gains_in[...]

    for k in range(nx):

        @pl.when(i == k)
        def _(k=k):
            x[...] = xs[k][...]

    u = x[...].astype(F32)
    r = lax.rsqrt(jnp.mean(u * u, axis=1, keepdims=True) + EPS)
    low = (u * r * gains[0:1, :]).astype(BF16)
    normed[...] = low
    y = mm(low, w[...])
    c = cos[...]
    s = sin[...]
    gq = gains[2:3, :HEAD]
    gk = gains[3:4, :HEAD]
    for h in range(kv_heads):
        base = h * (group + 2) * HEAD
        kept = h * (group + 1) * HEAD
        for j in range(group + 1):
            v = y[:, base + j * HEAD : base + (j + 1) * HEAD]
            raw[:, kept + j * HEAD : kept + (j + 1) * HEAD] = v
            scale = gq if j < group else gk
            v = v * lax.rsqrt(jnp.mean(v * v, axis=1, keepdims=True) + EPS) * scale
            v = v * c + pltpu.roll(v, HEAD // 2, 1) * s
            packed[:, base + j * HEAD : base + (j + 1) * HEAD] = v.astype(BF16)
        end = base + (group + 1) * HEAD
        packed[:, end : end + HEAD] = y[:, end : end + HEAD].astype(BF16)


def qkv_call(t, xs, ws, gains, packed_gains, cos, sin, width, kv_heads, group):
    rows = xs[0].shape[0]
    n = rows * len(xs)
    cols = kv_heads * (group + 2) * HEAD
    kept = kv_heads * (group + 1) * HEAD
    return call(
        functools.partial(qkv_kernel, len(xs), len(ws), packed_gains, kv_heads, group),
        (len(xs),),
        [part_at((rows, width), 0) for _ in xs]
        + [part_at((w.shape[0], cols), 0) for w in ws]
        + [whole(gains.shape), rows_xor(rows, HEAD), rows_xor(rows, HEAD)],
        [rows_at(rows, width), rows_xor(rows, cols), rows_xor(rows, kept), whole((8, width))],
        [
            shape_of((n, width)),
            shape_of((n, cols)),
            shape_of((n, kept), F32),
            shape_of((8, width), F32),
        ],
        2 * n * width * cols,
        [pltpu.VMEM((width, cols), BF16), pltpu.VMEM((rows, width), BF16)],
    )(t, *xs, *ws, gains, cos, sin)


def weights_of(q, k, same, causal):
    e = jnp.exp2(mm(k, q, 1, 1) * EXP2_SCALE)
    keep = same if causal is None else same & causal
    return jnp.where(keep, e, 0.0)


def accumulate(part, acc):
    h = pl.program_id(0)

    @pl.when(h == 0)
    def _():
        acc[...] = part

    @pl.when(h > 0)
    def _():
        acc[...] += part


def split_rows(rows, acc, keep, send):
    for k in range(acc.shape[0] // rows):
        out = send if k % 2 else keep
        at = (k // 2) * rows
        out[at : at + rows, :] = acc[k * rows : (k + 1) * rows, :].astype(BF16)


def attn_forward_kernel(rows, blocks, group, kv_heads, nw, t, packed, seg_col, seg_row, *refs):
    ws = refs[:nw]
    mixed, inv, keep, send, w, acc = refs[nw:]
    causal = lax.broadcasted_iota(jnp.int32, (rows, rows), 0) <= lax.broadcasted_iota(
        jnp.int32, (rows, rows), 1
    )
    kc = group * HEAD
    join(ws, w)
    for i in range(blocks):
        lo = i * rows
        at = pl.multiple_of(lax.bitwise_xor(i, t[0]) * rows, rows)
        sq = seg_row[:, lo : lo + rows]
        for j in range(group):
            q = packed[lo : lo + rows, j * HEAD : (j + 1) * HEAD]
            parts = []
            total = jnp.zeros((1, rows), F32)
            for b in range(i + 1):
                k = packed[b * rows : (b + 1) * rows, kc : kc + HEAD]
                same = seg_col[b * rows : (b + 1) * rows, :] == sq
                e = weights_of(q, k, same, causal if b == i else None)
                total = total + jnp.sum(e, axis=0, keepdims=True)
                parts.append(e)
            rec = 1.0 / total
            inv[0, j : j + 1, lo : lo + rows] = rec
            out = jnp.zeros((rows, HEAD), F32)
            for b in range(i + 1):
                v = packed[b * rows : (b + 1) * rows, kc + HEAD : kc + 2 * HEAD]
                out = out + mm((parts[b] * rec).astype(BF16), v, 0, 0)
            mixed[pl.ds(at, rows), j * HEAD : (j + 1) * HEAD] = out.astype(BF16)
    accumulate(mm(mixed[...], w[...], 1, 1), acc)

    @pl.when(pl.program_id(0) == kv_heads - 1)
    def _():
        split_rows(rows, acc, keep, send)


def by_head(n, width, first=0):
    return pl.BlockSpec((n, width), lambda h, t: (0, first + h))


def attn_forward(t, packed, seg_col, seg_row, w_o, first, rows, width, kv_heads, group):
    n = packed.shape[0]
    q_cols = group * HEAD
    return call(
        functools.partial(attn_forward_kernel, rows, n // rows, group, kv_heads, len(w_o)),
        (kv_heads,),
        [by_head(n, q_cols + 2 * HEAD), whole(seg_col.shape), whole(seg_row.shape)]
        + [by_head(w.shape[0], q_cols, first) for w in w_o],
        [
            by_head(n, q_cols),
            pl.BlockSpec((1, 8, n), lambda h, t: (h, 0, 0)),
            whole((n // 2, width)),
            whole((n // 2, width)),
        ],
        [
            shape_of((n, kv_heads * q_cols)),
            shape_of((kv_heads, 8, n), F32),
            shape_of((n // 2, width)),
            shape_of((n // 2, width)),
        ],
        kv_heads * group * n * n * HEAD * 4,
        [pltpu.VMEM((width, q_cols), BF16), pltpu.VMEM((n, width), F32)],
    )(t, packed, seg_col, seg_row, *w_o)


def head_back(e, u, cos, sin, gain):
    e = e * cos - pltpu.roll(e, HEAD // 2, 1) * sin
    r = lax.rsqrt(jnp.mean(u * u, axis=1, keepdims=True) + EPS)
    ur = u * r
    dgain = jnp.sum(e * ur, axis=0, keepdims=True)
    ec = e * gain
    du = r * (ec - ur * jnp.mean(ur * ec, axis=1, keepdims=True))
    return du, dgain


def fill_gain_rows(d_attn, d_mlp, d_heads, outs):
    n = outs[0].shape[0] // GAIN_ROWS
    at = lax.broadcasted_iota(jnp.int32, (GAIN_ROWS, 4 * HEAD), 0)
    for k, out in enumerate(outs):
        out[...] = jnp.zeros_like(out)
        for p in range(n):
            here = slice((k * n + p) * HEAD, (k * n + p + 1) * HEAD)
            row = jnp.concatenate(
                [d_attn[0:1, here], d_mlp[0:1, here], d_heads[0:1], d_heads[1:2]], axis=1
            )
            rows = slice(p * GAIN_ROWS, (p + 1) * GAIN_ROWS)
            out[rows, : 4 * HEAD] = jnp.where(at == 0, row, 0.0).astype(BF16)


def attn_backward_kernel(rows, blocks, group, kv_heads, nw, packed_gains, t, *refs):
    packed, seg_col, seg_row, inv, raw, cos, sin, gains, dgain_mlp = refs[:9]
    refs = refs[9:]
    branch, refs = refs[:blocks], refs[blocks:]
    xs, refs = refs[:blocks], refs[blocks:]
    w_os, refs = refs[:nw], refs[nw:]
    w_qkvs, refs = refs[:nw], refs[nw:]
    dpacked, dgain, keep, send, dgain_x, *tails, dk, dv, dmix, w_o, w_qkv, acc, heads = refs
    causal = lax.broadcasted_iota(jnp.int32, (rows, rows), 0) <= lax.broadcasted_iota(
        jnp.int32, (rows, rows), 1
    )
    kc = group * HEAD
    gq = gains[2:3, :HEAD]
    gk = gains[3:4, :HEAD]
    join(w_os, w_o)
    join(w_qkvs, w_qkv)
    for k in range(blocks):
        dmix[k * rows : (k + 1) * rows, :] = mm(branch[k][...], w_o[...]).astype(BF16)
    dk[...] = jnp.zeros_like(dk)
    dv[...] = jnp.zeros_like(dv)
    dgain[...] = jnp.zeros_like(dgain)
    for i in range(blocks):
        lo = i * rows
        at = pl.multiple_of(lax.bitwise_xor(i, t[0]) * rows, rows)
        sq = seg_row[:, lo : lo + rows]
        for j in range(group):
            q = packed[lo : lo + rows, j * HEAD : (j + 1) * HEAD]
            do = dmix[pl.ds(at, rows), j * HEAD : (j + 1) * HEAD]
            rec = inv[0, j : j + 1, lo : lo + rows]
            probs = []
            dprobs = []
            delta = jnp.zeros((1, rows), F32)
            for b in range(i + 1):
                here = slice(b * rows, (b + 1) * rows)
                k = packed[here, kc : kc + HEAD]
                v = packed[here, kc + HEAD : kc + 2 * HEAD]
                same = seg_col[here, :] == sq
                p = weights_of(q, k, same, causal if b == i else None) * rec
                dp = mm(v, do, 1, 1)
                delta = delta + jnp.sum(p * dp, axis=0, keepdims=True)
                dv[here, :] += mm(p.astype(BF16), do)
                probs.append(p)
                dprobs.append(dp)
            dq = jnp.zeros((rows, HEAD), F32)
            for b in range(i + 1):
                here = slice(b * rows, (b + 1) * rows)
                k = packed[here, kc : kc + HEAD]
                ds = (probs[b] * (dprobs[b] - delta)).astype(BF16)
                dk[here, :] += mm(ds, q)
                dq = dq + mm(ds, k, 0, 0)
            du, dg = head_back(
                dq * SCALE,
                raw[lo : lo + rows, j * HEAD : (j + 1) * HEAD],
                cos[lo : lo + rows, :],
                sin[lo : lo + rows, :],
                gq,
            )
            dgain[0, 0:1, :] += dg
            dpacked[pl.ds(at, rows), j * HEAD : (j + 1) * HEAD] = du.astype(BF16)
    for i in range(blocks):
        here = slice(i * rows, (i + 1) * rows)
        at = pl.multiple_of(lax.bitwise_xor(i, t[0]) * rows, rows)
        du, dg = head_back(
            dk[here, :] * SCALE, raw[here, kc : kc + HEAD], cos[here, :], sin[here, :], gk
        )
        dgain[0, 1:2, :] += dg
        dpacked[pl.ds(at, rows), kc : kc + HEAD] = du.astype(BF16)
        dpacked[pl.ds(at, rows), kc + HEAD : kc + 2 * HEAD] = dv[here, :].astype(BF16)
    accumulate(mm(dpacked[...], w_qkv[...], 1, 1), acc)
    accumulate(dgain[0], heads)

    @pl.when(pl.program_id(0) == kv_heads - 1)
    def _():
        total = jnp.zeros((1, acc.shape[1]), F32)
        for k in range(blocks):
            u = xs[k][...].astype(F32)
            ur = u * lax.rsqrt(jnp.mean(u * u, axis=1, keepdims=True) + EPS)
            total = total + jnp.sum(acc[k * rows : (k + 1) * rows, :] * ur, axis=0, keepdims=True)
        dgain_x[...] = jnp.broadcast_to(total, dgain_x.shape)
        if packed_gains:
            fill_gain_rows(dgain_x, dgain_mlp, heads[...], tails)
        split_rows(rows, acc, keep, send)


def attn_backward(
    t,
    packed_gains,
    packed,
    seg_col,
    seg_row,
    inv,
    raw,
    cos,
    sin,
    gains,
    dgain_mlp,
    branch,
    xs,
    w_o,
    first,
    w_qkv,
    width,
    kv_heads,
    group,
):
    n = packed.shape[0]
    rows = xs[0].shape[0]
    q_cols = group * HEAD
    cols = q_cols + 2 * HEAD
    tails = [(len(w_o) // 2 * GAIN_ROWS, kv_heads * cols)] * 2 if packed_gains else []
    return call(
        functools.partial(
            attn_backward_kernel, rows, n // rows, group, kv_heads, len(w_o), packed_gains
        ),
        (kv_heads,),
        [
            by_head(n, cols),
            whole(seg_col.shape),
            whole(seg_row.shape),
            pl.BlockSpec((1, 8, n), lambda h, t: (h, 0, 0)),
            by_head(n, q_cols + HEAD),
            whole(cos.shape),
            whole(sin.shape),
            whole(gains.shape),
            whole(dgain_mlp.shape),
        ]
        + [whole(b.shape) for b in branch]
        + [part_at((rows, width), 0) for _ in xs]
        + [by_head(w.shape[0], q_cols, first) for w in w_o]
        + [by_head(w.shape[0], cols) for w in w_qkv],
        [
            by_head(n, cols),
            pl.BlockSpec((1, 8, HEAD), lambda h, t: (h, 0, 0)),
            whole((n // 2, width)),
            whole((n // 2, width)),
            whole((8, width)),
        ]
        + [whole(shape) for shape in tails],
        [
            shape_of(packed.shape),
            shape_of((kv_heads, 8, HEAD), F32),
            shape_of((n // 2, width)),
            shape_of((n // 2, width)),
            shape_of((8, width), F32),
        ]
        + [shape_of(shape) for shape in tails],
        kv_heads * group * n * n * HEAD * 10,
        [
            pltpu.VMEM((n, HEAD), F32),
            pltpu.VMEM((n, HEAD), F32),
            pltpu.VMEM((n, q_cols), BF16),
            pltpu.VMEM((width, q_cols), BF16),
            pltpu.VMEM((width, cols), BF16),
            pltpu.VMEM((n, width), F32),
            pltpu.VMEM((8, HEAD), F32),
        ],
    )(t, packed, seg_col, seg_row, inv, raw, cos, sin, gains, dgain_mlp, *branch, *xs, *w_o, *w_qkv)


def join_in_order(t, reorder, block, out):
    if not reorder:
        out[...] = block[...]
        return
    for p in range(out.shape[0] // HEAD):
        out[p * HEAD : (p + 1) * HEAD, :] = block[pl.ds(model_block(t, p), HEAD), :]


def mlp_kernel(ff, nx, reorder, t, *refs):
    xs, refs = refs[:nx], refs[nx:]
    gs, refs = refs[:nx], refs[nx:]
    w_gu, w_d, *refs = refs
    act, dgu, x_out, g_out, dx_keep, dx_send, out_keep, out_send, w, wd, x, g = refs
    i = pl.program_id(0)

    @pl.when(i == 0)
    def _():
        join_in_order(t, reorder, w_gu, w)
        join_in_order(t, reorder, w_d, wd)

    for k in range(nx):

        @pl.when(i == k)
        def _(k=k):
            x[...] = xs[k][...]
            g[...] = gs[k][...]
            store_columns(t, reorder, xs[k][...], x_out)
            g_out[...] = gs[k][...]

    y = mm(x[...], w[...])
    gate = y[:, :ff]
    up = y[:, ff:]
    sig = 1.0 / (1.0 + jnp.exp(-gate))
    silu = gate * sig
    a = (silu * up).astype(BF16)
    act[...] = a
    da = mm(g[...], wd[...])
    dgu[:, :ff] = (da * up * sig * (1.0 + gate * (1.0 - sig))).astype(BF16)
    dgu[:, ff:] = (da * silu).astype(BF16)
    dx = mm(dgu[...], w[...], 1, 1).astype(BF16)
    out = mm(a, wd[...], 1, 1).astype(BF16)

    @pl.when(lax.rem(i, 2) == 0)
    def _():
        dx_keep[...] = dx
        out_keep[...] = out

    @pl.when(lax.rem(i, 2) == 1)
    def _():
        dx_send[...] = dx
        out_send[...] = out


def mlp_call(t, reorder, xs, gs, g_index, w_gu, w_d, d_index, ff, width):
    rows = xs[0].shape[0]
    n = rows * len(xs)
    halves = pl.BlockSpec((rows, width), lambda i, t: (lax.div(i, 2), 0))
    return call(
        functools.partial(mlp_kernel, ff, len(xs), reorder),
        (len(xs),),
        [whole(x.shape) for x in xs]
        + [part_at((rows, width), g_index) for _ in gs]
        + [part_at((width, 2 * ff), 0), part_at((width, ff), d_index)],
        [rows_at(rows, ff), rows_at(rows, 2 * ff)] + [rows_at(rows, width)] * 2 + [halves] * 4,
        [shape_of((n, ff)), shape_of((n, 2 * ff))]
        + [shape_of((n, width))] * 2
        + [shape_of((n // 2, width))] * 4,
        2 * n * width * ff * 6,
        [
            pltpu.VMEM((width, 2 * ff), BF16),
            pltpu.VMEM((width, ff), BF16),
            pltpu.VMEM((rows, width), BF16),
            pltpu.VMEM((rows, width), BF16),
        ],
    )(t, *xs, *gs, w_gu, w_d)


def sum_of(parts):
    total = parts[0][...].astype(F32)
    for p in parts[1:]:
        total = total + p[...].astype(F32)
    return total


def hidden_kernel(n_parts, t, *refs):
    parts = refs[:n_parts]
    x, gains, hidden, normed = refs[n_parts:]
    h = x[...].astype(F32) + sum_of(parts)
    hidden[...] = h
    r = lax.rsqrt(jnp.mean(h * h, axis=1, keepdims=True) + EPS)
    normed[...] = (h * r * gains[1:2, :]).astype(BF16)


def row_tile(rows, width, index=0):
    return pl.BlockSpec((rows // ROW_STEPS, width), lambda i, t: (i, index))


def hidden_call(t, parts, x, gains, rows, width):
    spec = row_tile(rows, width)
    return call(
        functools.partial(hidden_kernel, len(parts)),
        (ROW_STEPS,),
        [spec for _ in parts] + [spec, whole(gains.shape)],
        [spec, spec],
        [shape_of((rows, width), F32), shape_of((rows, width))],
        rows * width * 8,
    )(t, *parts, x, gains)


def norm_back(e, u, gain):
    r = lax.rsqrt(jnp.mean(u * u, axis=1, keepdims=True) + EPS)
    ur = u * r
    ec = e * gain
    return r * (ec - ur * jnp.mean(ur * ec, axis=1, keepdims=True)), jnp.sum(e * ur, axis=0, keepdims=True)


def d_hidden_kernel(n_parts, t, *refs):
    parts = refs[:n_parts]
    hidden, g, gains, d_hidden, branch, d_gain = refs[n_parts:]
    du, dg = norm_back(sum_of(parts), hidden[...], gains[1:2, :])
    d = g[...].astype(F32) + du
    d_hidden[...] = d
    branch[...] = d.astype(BF16)
    accumulate(jnp.broadcast_to(dg, d_gain.shape), d_gain)


def d_hidden_call(t, parts, hidden, g, g_index, gains, rows, width):
    spec = row_tile(rows, width)
    return call(
        functools.partial(d_hidden_kernel, len(parts)),
        (ROW_STEPS,),
        [spec for _ in parts] + [spec, row_tile(rows, width, g_index), whole(gains.shape)],
        [spec, spec, whole((8, width))],
        [shape_of((rows, width), F32), shape_of((rows, width)), shape_of((8, width), F32)],
        rows * width * 12,
    )(t, *parts, hidden, g, gains)


def store_columns(t, reorder, value, out):
    if not reorder:
        out[...] = value
        return
    for p in range(value.shape[1] // HEAD):
        out[:, pl.ds(model_block(t, p), HEAD)] = value[:, p * HEAD : (p + 1) * HEAD]


def activations_kernel(n_parts, reorder, t, *refs):
    parts = refs[:n_parts]
    hidden, out = refs[n_parts:]
    store_columns(t, reorder, (hidden[...] + sum_of(parts)).astype(BF16), out)


def activations_call(t, reorder, parts, hidden, rows, width):
    spec = row_tile(rows, width)
    return call(
        functools.partial(activations_kernel, len(parts), reorder),
        (ROW_STEPS,),
        [spec for _ in parts] + [spec],
        spec,
        shape_of((rows, width)),
        rows * width * 2,
    )(t, *parts, hidden)


def d_tokens_kernel(n_parts, reorder, t, *refs):
    parts = refs[:n_parts]
    x, d_hidden, gains, out = refs[n_parts:]
    du, _ = norm_back(sum_of(parts), x[...].astype(F32), gains[0:1, :])
    store_columns(t, reorder, d_hidden[...] + du, out)


def d_tokens_call(t, reorder, parts, x, d_hidden, gains, rows, width):
    spec = row_tile(rows, width)
    return call(
        functools.partial(d_tokens_kernel, len(parts), reorder),
        (ROW_STEPS,),
        [spec for _ in parts] + [spec, spec, whole(gains.shape)],
        spec,
        shape_of((rows, width), F32),
        rows * width * 12,
    )(t, *parts, x, d_hidden, gains)


def outer_half(left, right, half):
    m = left.shape[1] // 2
    return mm(left[:, half * m : (half + 1) * m], right, 0, 0).astype(BF16)


def shard_of(parts):
    total = parts[0].astype(F32)
    for p in parts[1:]:
        total = total + p.astype(F32)
    return total


def unpack_heads(kv_heads, group, w):
    q, k, v = [], [], []
    for h in range(kv_heads):
        base = h * (group + 2) * HEAD
        mid = base + group * HEAD
        q.append(w[:, base:mid])
        k.append(w[:, mid : mid + HEAD])
        v.append(w[:, mid + HEAD : mid + 2 * HEAD])
    join = lambda parts: jnp.concatenate(parts, axis=1)
    return join(q), join(k), join(v)


def pair_sum_kernel(t, keep, rows, got, *outs):
    n = keep.shape[0] // len(outs)
    for z, out in enumerate(outs):
        here = slice(z * n, (z + 1) * n)
        low = slice(z * GAIN_ROWS, (z + 1) * GAIN_ROWS)
        there = slice(keep.shape[0] + z * GAIN_ROWS, keep.shape[0] + (z + 1) * GAIN_ROWS)
        out[:n, :] = (keep[here, :].astype(F32) + got[here, :].astype(F32)).astype(out.dtype)
        out[n:, :] = (rows[low, :].astype(F32) + got[there, :].astype(F32)).astype(out.dtype)


def pair_sum(t, keep, rows, got, parts):
    m, cols = keep.shape
    n = m // parts + GAIN_ROWS
    return call(
        pair_sum_kernel,
        (1,),
        [whole(keep.shape), whole(rows.shape), whole(got.shape)],
        [whole((n, cols)) for _ in range(parts)],
        [shape_of((n, cols), F32 if z == 0 else BF16) for z in range(parts)],
        m * cols,
    )(t, keep, rows, got)


def xor_pairs(size, bits):
    return [(i, i ^ bits) for i in range(size)]


class Links:
    def __init__(self, dp, tensor):
        self.dp, self.tensor = dp, tensor
        self.direct = (dp, tensor) == (8, 4)
        self.d = lax.axis_index("dp")
        self.t = lax.axis_index("tensor")

    def over_dp(self, x, bits):
        return lax.ppermute(x, "dp", xor_pairs(self.dp, bits))

    def over_tensor(self, x, bits):
        return lax.ppermute(x, "tensor", xor_pairs(self.tensor, bits))

    def offsets(self):
        if self.direct:
            return jnp.stack([self.t, self.d])
        return jnp.zeros((2,), jnp.int32)

    def gather_dp(self, x):
        if not self.direct:
            return [lax.all_gather(x, "dp", axis=0, tiled=True)]
        own = self.gather_z(x)
        return own + [self.over_dp(b, 1) for b in own]

    def gather_z(self, x):
        return [x] + [self.over_dp(x, 2 * z) for z in (1, 2, 3)]

    def send_half(self, left, right):
        send = outer_half(left, right, 1)
        if self.direct:
            send = self.over_dp(send, 1)
        return send, outer_half(left, right, 0)

    def send_quarters(self, got, keep):
        if not self.direct:
            both = jnp.concatenate([keep, got], axis=0)
            return [lax.psum_scatter(both, "dp", scatter_dimension=0, tiled=True)]
        n = keep.shape[0] // 4
        part = lambda z: keep[z * n : (z + 1) * n].astype(F32) + got[z * n : (z + 1) * n].astype(F32)
        return [part(0)] + [self.over_dp(part(z).astype(BF16), 2 * z) for z in (1, 2, 3)]

    def gather_tensor(self, x, *after):
        if not self.direct:
            full = lax.all_gather(x, "tensor", axis=0, tiled=True)
            return jnp.split(full, self.tensor, axis=0)
        far = self.over_tensor(x, 2)
        return [x, self.over_tensor(x, 1), far, self.over_tensor(tie(far, *after) if after else far, 1)]

    def scatter_tensor(self, keep, send, sent=False):
        rows = 2 * keep.shape[0] // self.tensor
        if not self.direct:
            blocks = []
            for k in range(self.tensor // 2):
                blocks += [keep[k * rows : (k + 1) * rows], send[k * rows : (k + 1) * rows]]
            full = jnp.concatenate(blocks, axis=0)
            return [lax.psum_scatter(full, "tensor", scatter_dimension=0, tiled=True)]
        got = send if sent else self.over_tensor(send, 1)
        far = keep[rows:].astype(F32) + got[rows:].astype(F32)
        far = far.astype(BF16)
        return [keep, got, self.over_tensor(far, 2), far]


def rope_tables(offsets):
    frequency = ROPE_BASE ** (-(2.0 * jnp.arange(HEAD // 2, dtype=F32)) / HEAD)
    angles = offsets.astype(F32)[:, None] * frequency[None, :]
    cos, sin = jnp.cos(angles), jnp.sin(angles)
    return jnp.concatenate([cos, cos], axis=1), jnp.concatenate([-sin, sin], axis=1)


def pack_heads(wq, wk, wv, group):
    parts = []
    for h in range(wk.shape[1] // HEAD):
        parts += [
            wq[:, h * group * HEAD : (h + 1) * group * HEAD],
            wk[:, h * HEAD : (h + 1) * HEAD],
            wv[:, h * HEAD : (h + 1) * HEAD],
        ]
    return jnp.concatenate(parts, axis=1)


def body(
    dp,
    tensor,
    tokens,
    segment_ids,
    positions,
    w_query,
    key_projection,
    value_projection,
    w_out,
    w_gate,
    w_up,
    w_down,
    gain_attn,
    gain_mlp,
    gain_query,
    gain_key,
    cotangent,
):
    links = Links(dp, tensor)
    direct = links.direct
    rows, width = tokens.shape
    kv_heads = key_projection.shape[1] // HEAD
    group = w_query.shape[1] // key_projection.shape[1]
    q_cols = group * HEAD
    ff = w_gate.shape[1]
    head_part = HEAD // dp
    t = links.offsets()

    if direct:
        w_attn = pack_attn(
            t,
            w_query,
            key_projection,
            value_projection,
            w_out,
            (gain_attn, gain_mlp, gain_query, gain_key),
            kv_heads,
            group,
        )
        both = pack_rows(t, tie(tokens, w_attn), cotangent)
        w_mlp = pack_mlp(t, tie(w_gate, both), w_up, w_down)
        attn_near = links.gather_z(w_attn)
        attn_far = links.over_dp(w_attn, 1)
        beside = links.over_tensor(both, 1)
        far = links.over_tensor(both, 2)
        across = tie(far, attn_far, attn_near[1], attn_near[2])
        rows_all = [both, beside, far, links.over_tensor(across, 1)]
        w_attn = attn_near + [attn_far] + [links.over_dp(b, 1) for b in attn_near[1:]]
        w_mlp = tie(w_mlp, (far, attn_far, attn_near[1:], w_attn[5], w_attn[6]))
        w_qkv, w_o, o_index = w_attn, w_attn, kv_heads * (group + 2) * HEAD // q_cols
        w_gu = w_d = lax.all_gather(w_mlp, "dp", axis=0, tiled=True)
        d_index = 2
        gains = jnp.zeros((8, width), F32)
    else:
        w_qkv = links.gather_dp(pack_heads(w_query, key_projection, value_projection, group))
        w_o = links.gather_dp(w_out.T)
        w_gu = links.gather_dp(jnp.concatenate([w_gate, w_up], axis=1))[0]
        w_d = links.gather_dp(w_down.T)[0]
        d_index, o_index = 0, 0
        row = lambda g: jnp.pad(g, (0, width - g.shape[0]))[None, :].astype(F32)
        whole_gain = lambda g: row(lax.all_gather(g, "dp", axis=0, tiled=True))
        gains = jnp.concatenate(
            [whole_gain(g) for g in (gain_attn, gain_mlp, gain_query, gain_key)]
            + [jnp.zeros((4, width), F32)],
            axis=0,
        )
        rows_all = links.gather_tensor(jnp.concatenate([tokens, cotangent], axis=1))
    own = rows_all[0] if direct else jnp.concatenate([tokens, cotangent], axis=1)

    cos, sin = rope_tables(positions[0])
    seg_row = segment_ids
    seg_col = segment_ids.reshape(-1, 1)

    normed, packed, raw, gains = qkv_call(
        t, rows_all, w_qkv, gains, direct, cos, sin, width, kv_heads, group
    )
    mixed, inv, keep, send = attn_forward(
        t, packed, seg_col, seg_row, w_o, o_index, rows, width, kv_heads, group
    )
    parts = links.scatter_tensor(keep, send)
    hidden, normed_mlp = hidden_call(t, parts[:3], own, gains, rows, width)
    normed_mlp = links.gather_tensor(normed_mlp)
    act, d_gu, normed_mlp, cot, dx_keep, dx_send, out_keep, out_send = mlp_call(
        t, direct, normed_mlp, rows_all, 1, w_gu, w_d, d_index, ff, width
    )
    parts = links.scatter_tensor(dx_keep, dx_send)
    down = links.send_half(cot, tie(act, parts[1:2]))
    d_hidden, branch, d_gain_mlp = d_hidden_call(t, parts[:3], hidden, own, 1, gains, rows, width)
    gu_sum = mm(normed_mlp, tie(d_gu, branch), 0, 0).astype(BF16)
    gu = lax.psum_scatter(gu_sum, "dp", scatter_dimension=0, tiled=True)
    branch = links.gather_tensor(branch, gu_sum, down[0])
    down = links.send_quarters(*down)
    out_parts = links.scatter_tensor(out_keep, tie(out_send, branch))[:3]
    branch_rows = jnp.concatenate(branch, axis=0)
    out_sent = outer_half(branch_rows, mixed, 1)
    if direct:
        out_sent = links.over_dp(out_sent, 1)
    d_packed, d_gain_heads, keep, send, d_gain_attn, *tails = tie(
        attn_backward(
            t, direct, packed, seg_col, seg_row, inv, raw, cos, sin, gains, d_gain_mlp, branch, rows_all,
            w_o, o_index, w_qkv, width, kv_heads, group,
        ),
        out_sent,
        down[1:],
        out_parts,
    )
    if direct:
        send_qkv = jnp.concatenate([outer_half(normed, d_packed, 1), tails[1]], axis=0)
        got = links.over_dp(send_qkv, 1)
    parts = links.scatter_tensor(keep, send)[:3]
    out = (out_sent, outer_half(branch_rows, tie(mixed, parts[:2]), 0))
    out = links.send_quarters(*tie(out, parts[:2]))
    if direct:
        keep_qkv = outer_half(normed, d_packed, 0)
        qkv = pair_sum(t, keep_qkv, tails[0], tie(got, out[1:], parts[2]), 4)
        qkv = [qkv[0]] + [links.over_dp(qkv[z], 2 * z) for z in (1, 2, 3)]
    else:
        qkv = links.send_quarters(*links.send_half(normed, d_packed))
    d_tokens = d_tokens_call(t, direct, parts, own, d_hidden, gains, rows, width)
    activations = activations_call(t, direct, out_parts, hidden, rows, width)
    grad_down = shard_of(down).T
    grad_gate, grad_up = gu[:, :ff].astype(F32), gu[:, ff:].astype(F32)
    grad_out = shard_of(out).T
    n = width // dp
    qkv = shard_of(qkv)
    grad_query, grad_key, grad_value = unpack_heads(kv_heads, group, qkv[:n])
    if direct:
        sums = qkv[n : n + 1, : 4 * HEAD]
        sums = sums + links.over_tensor(sums, 1)
        sums = (sums + links.over_tensor(sums, 2)).reshape(4, HEAD)
        sum_attn, sum_mlp, sum_query, sum_key = sums[0], sums[1], sums[2], sums[3]
    else:
        heads = jnp.sum(d_gain_heads, axis=0)
        sum_attn, sum_mlp, sum_query, sum_key = lax.psum(
            (d_gain_attn[0], d_gain_mlp[0], heads[0], heads[1]), ("dp", "tensor")
        )
        sum_attn = lax.dynamic_slice_in_dim(sum_attn, links.d * n, n, 0)
        sum_mlp = lax.dynamic_slice_in_dim(sum_mlp, links.d * n, n, 0)
    shard = lambda v: lax.dynamic_slice_in_dim(v, links.d * head_part, head_part, 0)
    return (
        activations,
        d_tokens,
        grad_query,
        grad_key,
        grad_value,
        grad_out,
        grad_gate,
        grad_up,
        grad_down,
        sum_attn,
        sum_mlp,
        shard(sum_query),
        shard(sum_key),
    )


def solution(mesh):
    tokens = P(("dp", "tensor"), None)
    by_rows = P("dp", "tensor")
    by_columns = P("tensor", "dp")
    sequence = P("dp", None)
    gain = P("dp")
    return jax.shard_map(
        functools.partial(body, mesh.shape["dp"], mesh.shape["tensor"]),
        mesh=mesh,
        in_specs=(
            tokens,
            sequence,
            sequence,
            by_rows,
            by_rows,
            by_rows,
            by_columns,
            by_rows,
            by_rows,
            by_columns,
            gain,
            gain,
            gain,
            gain,
            tokens,
        ),
        out_specs=(
            tokens,
            tokens,
            by_rows,
            by_rows,
            by_rows,
            by_columns,
            by_rows,
            by_rows,
            by_columns,
            gain,
            gain,
            gain,
            gain,
        ),
        check_vma=False,
    )
```

```python
import functools

import jax
import jax.numpy as jnp
from jax import lax
from jax.experimental import pallas as pl
from jax.experimental.pallas import tpu as pltpu
from jax.sharding import PartitionSpec as P

HEAD = 128
EPS = 1e-06
ROPE_BASE = 1000000.0
SCALE = HEAD ** (-0.5)
EXP2_SCALE = SCALE * 1.4426950408889634
F32 = jnp.float32
BF16 = jnp.bfloat16
VMEM_LIMIT = 60 * 1024 * 1024
ORDER = (0, 2, 4, 6, 1, 3, 5, 7)
GAIN_ROWS = 16
ROW_STEPS = 1


def mm(a, b, ca=1, cb=0):
    return lax.dot_general(a, b, (((ca,), (cb,)), ((), ())), preferred_element_type=F32)


def shape_of(shape, dtype=BF16):
    return jax.ShapeDtypeStruct(shape, dtype)


def call(kernel, grid, in_specs, out_specs, out_shape, flops, scratch=()):
    return pl.pallas_call(
        kernel,
        out_shape=out_shape,
        grid_spec=pltpu.PrefetchScalarGridSpec(
            num_scalar_prefetch=1,
            grid=grid,
            in_specs=in_specs,
            out_specs=out_specs,
            scratch_shapes=list(scratch),
        ),
        compiler_params=pltpu.CompilerParams(
            dimension_semantics=("arbitrary",) * len(grid), vmem_limit_bytes=VMEM_LIMIT
        ),
        cost_estimate=pl.CostEstimate(flops=1, bytes_accessed=1, transcendentals=0),
    )


def tie(x, *after):
    return lax.optimization_barrier((x, after))[0]


def whole(shape):
    return pl.BlockSpec(shape, lambda i, t: (0,) * len(shape))


def part_at(shape, index):
    return pl.BlockSpec(shape, lambda i, t: (0, index))


def rows_at(rows, cols):
    return pl.BlockSpec((rows, cols), lambda i, t: (i, 0))


def rows_xor(rows, cols):
    return pl.BlockSpec((rows, cols), lambda i, t: (lax.bitwise_xor(i, t[0]), 0))


def model_block(t, p):
    return pl.multiple_of(lax.bitwise_xor(t[1], ORDER[p]) * HEAD, HEAD)


def pack_attn_kernel(kv_heads, group, t, wq, wk, wv, wo, g_attn, g_mlp, g_query, g_key, out):
    n = wq.shape[0]
    for h in range(kv_heads):
        base = h * (group + 2) * HEAD
        mid = base + group * HEAD
        out[:n, base:mid] = wq[:, h * group * HEAD : (h + 1) * group * HEAD]
        out[:n, mid : mid + HEAD] = wk[:, h * HEAD : (h + 1) * HEAD]
        out[:n, mid + HEAD : mid + 2 * HEAD] = wv[:, h * HEAD : (h + 1) * HEAD]
    out[:n, kv_heads * (group + 2) * HEAD :] = wo[...].T
    out[n:, :] = jnp.zeros((GAIN_ROWS, out.shape[1]), BF16)
    m = g_query.shape[1]
    place = lax.broadcasted_iota(jnp.int32, (m, HEAD), 0) + t[1] * m == lax.broadcasted_iota(
        jnp.int32, (m, HEAD), 1
    )
    place = jnp.where(place, 1.0, 0.0).astype(BF16)
    rows = (g_attn[...].astype(F32), g_mlp[...].astype(F32), mm(g_query[...], place), mm(g_key[...], place))
    at = lax.broadcasted_iota(jnp.int32, (GAIN_ROWS, HEAD), 0)
    tile = jnp.zeros((GAIN_ROWS, HEAD), F32)
    for k, row in enumerate(rows):
        tile = jnp.where(at == k, row, tile)
    out[n:, :HEAD] = tile.astype(BF16)


def pack_attn(t, wq, wk, wv, wo, gains, kv_heads, group):
    n = wq.shape[0]
    cols = kv_heads * (group + 2) * HEAD + wo.shape[0]
    args = (wq, wk, wv, wo, *[g[None, :] for g in gains])
    return call(
        functools.partial(pack_attn_kernel, kv_heads, group),
        (1,),
        [whole(a.shape) for a in args],
        whole((n + GAIN_ROWS, cols)),
        shape_of((n + GAIN_ROWS, cols)),
        n * cols,
    )(t, *args)


def pack_rows_kernel(t, x, g, out):
    width = x.shape[1]
    for p in range(width // HEAD):
        at = model_block(t, p)
        out[:, p * HEAD : (p + 1) * HEAD] = x[:, pl.ds(at, HEAD)]
        out[:, width + p * HEAD : width + (p + 1) * HEAD] = g[:, pl.ds(at, HEAD)]


def pack_rows(t, x, g):
    n, width = x.shape
    return call(
        pack_rows_kernel,
        (1,),
        [whole(x.shape), whole(g.shape)],
        whole((n, 2 * width)),
        shape_of((n, 2 * width)),
        n * width,
    )(t, x, g)


def pack_mlp_kernel(t, wg, wu, wd, out):
    ff = wg.shape[1]
    out[:, :ff] = wg[...]
    out[:, ff : 2 * ff] = wu[...]
    out[:, 2 * ff :] = wd[...].T


def pack_mlp(t, wg, wu, wd):
    shape = (wg.shape[0], 3 * wg.shape[1])
    args = (wg, wu, wd)
    return call(
        pack_mlp_kernel,
        (1,),
        [whole(a.shape) for a in args],
        whole(shape),
        shape_of(shape),
        shape[0] * shape[1],
    )(t, *args)


def join(blocks, out):
    n = out.shape[0] // len(blocks)
    for p, b in enumerate(blocks):
        out[p * n : (p + 1) * n, :] = b[:n, :]


def qkv_kernel(nx, nw, packed_gains, kv_heads, group, t, *refs):
    xs, ws = refs[:nx], refs[nx : nx + nw]
    gains_in, cos, sin, normed, packed, raw, gains, w, x = refs[nx + nw :]
    i = pl.program_id(0)

    @pl.when(i == 0)
    def _():
        join(ws, w)
        if packed_gains:
            n = w.shape[0] // nw
            gains[...] = jnp.zeros_like(gains)
            heads = jnp.zeros((GAIN_ROWS, HEAD), F32)
            for p, b in enumerate(ws):
                tile = b[n:, :HEAD].astype(F32)
                gains[0:2, p * n : (p + 1) * n] = tile[0:2]
                heads = heads + tile
            gains[2:4, :HEAD] = heads[2:4]
        else:
            gains[...] = gains_in[...]

    for k in range(nx):

        @pl.when(i == k)
        def _(k=k):
            x[...] = xs[k][...]

    u = x[...].astype(F32)
    r = lax.rsqrt(jnp.mean(u * u, axis=1, keepdims=True) + EPS)
    low = (u * r * gains[0:1, :]).astype(BF16)
    normed[...] = low
    y = mm(low, w[...])
    c = cos[...]
    s = sin[...]
    gq = gains[2:3, :HEAD]
    gk = gains[3:4, :HEAD]
    for h in range(kv_heads):
        base = h * (group + 2) * HEAD
        kept = h * (group + 1) * HEAD
        for j in range(group + 1):
            v = y[:, base + j * HEAD : base + (j + 1) * HEAD]
            raw[:, kept + j * HEAD : kept + (j + 1) * HEAD] = v
            scale = gq if j < group else gk
            v = v * lax.rsqrt(jnp.mean(v * v, axis=1, keepdims=True) + EPS) * scale
            v = v * c + pltpu.roll(v, HEAD // 2, 1) * s
            packed[:, base + j * HEAD : base + (j + 1) * HEAD] = v.astype(BF16)
        end = base + (group + 1) * HEAD
        packed[:, end : end + HEAD] = y[:, end : end + HEAD].astype(BF16)


def qkv_call(t, xs, ws, gains, packed_gains, cos, sin, width, kv_heads, group):
    rows = xs[0].shape[0]
    n = rows * len(xs)
    cols = kv_heads * (group + 2) * HEAD
    kept = kv_heads * (group + 1) * HEAD
    return call(
        functools.partial(qkv_kernel, len(xs), len(ws), packed_gains, kv_heads, group),
        (len(xs),),
        [part_at((rows, width), 0) for _ in xs]
        + [part_at((w.shape[0], cols), 0) for w in ws]
        + [whole(gains.shape), rows_xor(rows, HEAD), rows_xor(rows, HEAD)],
        [rows_at(rows, width), rows_xor(rows, cols), rows_xor(rows, kept), whole((8, width))],
        [
            shape_of((n, width)),
            shape_of((n, cols)),
            shape_of((n, kept), F32),
            shape_of((8, width), F32),
        ],
        2 * n * width * cols,
        [pltpu.VMEM((width, cols), BF16), pltpu.VMEM((rows, width), BF16)],
    )(t, *xs, *ws, gains, cos, sin)


def weights_of(q, k, same, causal):
    e = jnp.exp2(mm(k, q, 1, 1) * EXP2_SCALE)
    keep = same if causal is None else same & causal
    return jnp.where(keep, e, 0.0)


def accumulate(part, acc):
    h = pl.program_id(0)

    @pl.when(h == 0)
    def _():
        acc[...] = part

    @pl.when(h > 0)
    def _():
        acc[...] += part


def split_rows(rows, acc, keep, send):
    for k in range(acc.shape[0] // rows):
        out = send if k % 2 else keep
        at = (k // 2) * rows
        out[at : at + rows, :] = acc[k * rows : (k + 1) * rows, :].astype(BF16)


def attn_forward_kernel(rows, blocks, group, kv_heads, nw, t, packed, seg_col, seg_row, *refs):
    ws = refs[:nw]
    mixed, inv, keep, send, w, acc = refs[nw:]
    causal = lax.broadcasted_iota(jnp.int32, (rows, rows), 0) <= lax.broadcasted_iota(
        jnp.int32, (rows, rows), 1
    )
    kc = group * HEAD
    join(ws, w)
    for i in range(blocks):
        lo = i * rows
        at = pl.multiple_of(lax.bitwise_xor(i, t[0]) * rows, rows)
        sq = seg_row[:, lo : lo + rows]
        for j in range(group):
            q = packed[lo : lo + rows, j * HEAD : (j + 1) * HEAD]
            parts = []
            total = jnp.zeros((1, rows), F32)
            for b in range(i + 1):
                k = packed[b * rows : (b + 1) * rows, kc : kc + HEAD]
                same = seg_col[b * rows : (b + 1) * rows, :] == sq
                e = weights_of(q, k, same, causal if b == i else None)
                total = total + jnp.sum(e, axis=0, keepdims=True)
                parts.append(e)
            rec = 1.0 / total
            inv[0, j : j + 1, lo : lo + rows] = rec
            out = jnp.zeros((rows, HEAD), F32)
            for b in range(i + 1):
                v = packed[b * rows : (b + 1) * rows, kc + HEAD : kc + 2 * HEAD]
                out = out + mm((parts[b] * rec).astype(BF16), v, 0, 0)
            mixed[pl.ds(at, rows), j * HEAD : (j + 1) * HEAD] = out.astype(BF16)
    accumulate(mm(mixed[...], w[...], 1, 1), acc)

    @pl.when(pl.program_id(0) == kv_heads - 1)
    def _():
        split_rows(rows, acc, keep, send)


def by_head(n, width, first=0):
    return pl.BlockSpec((n, width), lambda h, t: (0, first + h))


def attn_forward(t, packed, seg_col, seg_row, w_o, first, rows, width, kv_heads, group):
    n = packed.shape[0]
    q_cols = group * HEAD
    return call(
        functools.partial(attn_forward_kernel, rows, n // rows, group, kv_heads, len(w_o)),
        (kv_heads,),
        [by_head(n, q_cols + 2 * HEAD), whole(seg_col.shape), whole(seg_row.shape)]
        + [by_head(w.shape[0], q_cols, first) for w in w_o],
        [
            by_head(n, q_cols),
            pl.BlockSpec((1, 8, n), lambda h, t: (h, 0, 0)),
            whole((n // 2, width)),
            whole((n // 2, width)),
        ],
        [
            shape_of((n, kv_heads * q_cols)),
            shape_of((kv_heads, 8, n), F32),
            shape_of((n // 2, width)),
            shape_of((n // 2, width)),
        ],
        kv_heads * group * n * n * HEAD * 4,
        [pltpu.VMEM((width, q_cols), BF16), pltpu.VMEM((n, width), F32)],
    )(t, packed, seg_col, seg_row, *w_o)


def head_back(e, u, cos, sin, gain):
    e = e * cos - pltpu.roll(e, HEAD // 2, 1) * sin
    r = lax.rsqrt(jnp.mean(u * u, axis=1, keepdims=True) + EPS)
    ur = u * r
    dgain = jnp.sum(e * ur, axis=0, keepdims=True)
    ec = e * gain
    du = r * (ec - ur * jnp.mean(ur * ec, axis=1, keepdims=True))
    return du, dgain


def fill_gain_rows(d_attn, d_mlp, d_heads, outs):
    n = outs[0].shape[0] // GAIN_ROWS
    at = lax.broadcasted_iota(jnp.int32, (GAIN_ROWS, 4 * HEAD), 0)
    for k, out in enumerate(outs):
        out[...] = jnp.zeros_like(out)
        for p in range(n):
            here = slice((k * n + p) * HEAD, (k * n + p + 1) * HEAD)
            row = jnp.concatenate(
                [d_attn[0:1, here], d_mlp[0:1, here], d_heads[0:1], d_heads[1:2]], axis=1
            )
            rows = slice(p * GAIN_ROWS, (p + 1) * GAIN_ROWS)
            out[rows, : 4 * HEAD] = jnp.where(at == 0, row, 0.0).astype(BF16)


def attn_backward_kernel(rows, blocks, group, kv_heads, nw, packed_gains, t, *refs):
    packed, seg_col, seg_row, inv, raw, cos, sin, gains, dgain_mlp = refs[:9]
    refs = refs[9:]
    branch, refs = refs[:blocks], refs[blocks:]
    xs, refs = refs[:blocks], refs[blocks:]
    w_os, refs = refs[:nw], refs[nw:]
    w_qkvs, refs = refs[:nw], refs[nw:]
    dpacked, dgain, keep, send, dgain_x, *tails, dk, dv, dmix, w_o, w_qkv, acc, heads = refs
    causal = lax.broadcasted_iota(jnp.int32, (rows, rows), 0) <= lax.broadcasted_iota(
        jnp.int32, (rows, rows), 1
    )
    kc = group * HEAD
    gq = gains[2:3, :HEAD]
    gk = gains[3:4, :HEAD]
    join(w_os, w_o)
    join(w_qkvs, w_qkv)
    for k in range(blocks):
        dmix[k * rows : (k + 1) * rows, :] = mm(branch[k][...], w_o[...]).astype(BF16)
    dk[...] = jnp.zeros_like(dk)
    dv[...] = jnp.zeros_like(dv)
    dgain[...] = jnp.zeros_like(dgain)
    for i in range(blocks):
        lo = i * rows
        at = pl.multiple_of(lax.bitwise_xor(i, t[0]) * rows, rows)
        sq = seg_row[:, lo : lo + rows]
        for j in range(group):
            q = packed[lo : lo + rows, j * HEAD : (j + 1) * HEAD]
            do = dmix[pl.ds(at, rows), j * HEAD : (j + 1) * HEAD]
            rec = inv[0, j : j + 1, lo : lo + rows]
            probs = []
            dprobs = []
            delta = jnp.zeros((1, rows), F32)
            for b in range(i + 1):
                here = slice(b * rows, (b + 1) * rows)
                k = packed[here, kc : kc + HEAD]
                v = packed[here, kc + HEAD : kc + 2 * HEAD]
                same = seg_col[here, :] == sq
                p = weights_of(q, k, same, causal if b == i else None) * rec
                dp = mm(v, do, 1, 1)
                delta = delta + jnp.sum(p * dp, axis=0, keepdims=True)
                dv[here, :] += mm(p.astype(BF16), do)
                probs.append(p)
                dprobs.append(dp)
            dq = jnp.zeros((rows, HEAD), F32)
            for b in range(i + 1):
                here = slice(b * rows, (b + 1) * rows)
                k = packed[here, kc : kc + HEAD]
                ds = (probs[b] * (dprobs[b] - delta)).astype(BF16)
                dk[here, :] += mm(ds, q)
                dq = dq + mm(ds, k, 0, 0)
            du, dg = head_back(
                dq * SCALE,
                raw[lo : lo + rows, j * HEAD : (j + 1) * HEAD],
                cos[lo : lo + rows, :],
                sin[lo : lo + rows, :],
                gq,
            )
            dgain[0, 0:1, :] += dg
            dpacked[pl.ds(at, rows), j * HEAD : (j + 1) * HEAD] = du.astype(BF16)
    for i in range(blocks):
        here = slice(i * rows, (i + 1) * rows)
        at = pl.multiple_of(lax.bitwise_xor(i, t[0]) * rows, rows)
        du, dg = head_back(
            dk[here, :] * SCALE, raw[here, kc : kc + HEAD], cos[here, :], sin[here, :], gk
        )
        dgain[0, 1:2, :] += dg
        dpacked[pl.ds(at, rows), kc : kc + HEAD] = du.astype(BF16)
        dpacked[pl.ds(at, rows), kc + HEAD : kc + 2 * HEAD] = dv[here, :].astype(BF16)
    accumulate(mm(dpacked[...], w_qkv[...], 1, 1), acc)
    accumulate(dgain[0], heads)

    @pl.when(pl.program_id(0) == kv_heads - 1)
    def _():
        total = jnp.zeros((1, acc.shape[1]), F32)
        for k in range(blocks):
            u = xs[k][...].astype(F32)
            ur = u * lax.rsqrt(jnp.mean(u * u, axis=1, keepdims=True) + EPS)
            total = total + jnp.sum(acc[k * rows : (k + 1) * rows, :] * ur, axis=0, keepdims=True)
        dgain_x[...] = jnp.broadcast_to(total, dgain_x.shape)
        if packed_gains:
            fill_gain_rows(dgain_x, dgain_mlp, heads[...], tails)
        split_rows(rows, acc, keep, send)


def attn_backward(
    t,
    packed_gains,
    packed,
    seg_col,
    seg_row,
    inv,
    raw,
    cos,
    sin,
    gains,
    dgain_mlp,
    branch,
    xs,
    w_o,
    first,
    w_qkv,
    width,
    kv_heads,
    group,
):
    n = packed.shape[0]
    rows = xs[0].shape[0]
    q_cols = group * HEAD
    cols = q_cols + 2 * HEAD
    tails = [(len(w_o) // 2 * GAIN_ROWS, kv_heads * cols)] * 2 if packed_gains else []
    return call(
        functools.partial(
            attn_backward_kernel, rows, n // rows, group, kv_heads, len(w_o), packed_gains
        ),
        (kv_heads,),
        [
            by_head(n, cols),
            whole(seg_col.shape),
            whole(seg_row.shape),
            pl.BlockSpec((1, 8, n), lambda h, t: (h, 0, 0)),
            by_head(n, q_cols + HEAD),
            whole(cos.shape),
            whole(sin.shape),
            whole(gains.shape),
            whole(dgain_mlp.shape),
        ]
        + [whole(b.shape) for b in branch]
        + [part_at((rows, width), 0) for _ in xs]
        + [by_head(w.shape[0], q_cols, first) for w in w_o]
        + [by_head(w.shape[0], cols) for w in w_qkv],
        [
            by_head(n, cols),
            pl.BlockSpec((1, 8, HEAD), lambda h, t: (h, 0, 0)),
            whole((n // 2, width)),
            whole((n // 2, width)),
            whole((8, width)),
        ]
        + [whole(shape) for shape in tails],
        [
            shape_of(packed.shape),
            shape_of((kv_heads, 8, HEAD), F32),
            shape_of((n // 2, width)),
            shape_of((n // 2, width)),
            shape_of((8, width), F32),
        ]
        + [shape_of(shape) for shape in tails],
        kv_heads * group * n * n * HEAD * 10,
        [
            pltpu.VMEM((n, HEAD), F32),
            pltpu.VMEM((n, HEAD), F32),
            pltpu.VMEM((n, q_cols), BF16),
            pltpu.VMEM((width, q_cols), BF16),
            pltpu.VMEM((width, cols), BF16),
            pltpu.VMEM((n, width), F32),
            pltpu.VMEM((8, HEAD), F32),
        ],
    )(t, packed, seg_col, seg_row, inv, raw, cos, sin, gains, dgain_mlp, *branch, *xs, *w_o, *w_qkv)


def join_in_order(t, reorder, block, out):
    if not reorder:
        out[...] = block[...]
        return
    for p in range(out.shape[0] // HEAD):
        out[p * HEAD : (p + 1) * HEAD, :] = block[pl.ds(model_block(t, p), HEAD), :]


def mlp_kernel(ff, nx, reorder, t, *refs):
    xs, refs = refs[:nx], refs[nx:]
    gs, refs = refs[:nx], refs[nx:]
    w_gu, w_d, *refs = refs
    act, dgu, x_out, g_out, dx_keep, dx_send, out_keep, out_send, w, wd, x, g = refs
    i = pl.program_id(0)

    @pl.when(i == 0)
    def _():
        join_in_order(t, reorder, w_gu, w)
        join_in_order(t, reorder, w_d, wd)

    for k in range(nx):

        @pl.when(i == k)
        def _(k=k):
            x[...] = xs[k][...]
            g[...] = gs[k][...]
            store_columns(t, reorder, xs[k][...], x_out)
            g_out[...] = gs[k][...]

    y = mm(x[...], w[...])
    gate = y[:, :ff]
    up = y[:, ff:]
    sig = 1.0 / (1.0 + jnp.exp(-gate))
    silu = gate * sig
    a = (silu * up).astype(BF16)
    act[...] = a
    da = mm(g[...], wd[...])
    dgu[:, :ff] = (da * up * sig * (1.0 + gate * (1.0 - sig))).astype(BF16)
    dgu[:, ff:] = (da * silu).astype(BF16)
    dx = mm(dgu[...], w[...], 1, 1).astype(BF16)
    out = mm(a, wd[...], 1, 1).astype(BF16)

    @pl.when(lax.rem(i, 2) == 0)
    def _():
        dx_keep[...] = dx
        out_keep[...] = out

    @pl.when(lax.rem(i, 2) == 1)
    def _():
        dx_send[...] = dx
        out_send[...] = out


def mlp_call(t, reorder, xs, gs, g_index, w_gu, w_d, d_index, ff, width):
    rows = xs[0].shape[0]
    n = rows * len(xs)
    halves = pl.BlockSpec((rows, width), lambda i, t: (lax.div(i, 2), 0))
    return call(
        functools.partial(mlp_kernel, ff, len(xs), reorder),
        (len(xs),),
        [whole(x.shape) for x in xs]
        + [part_at((rows, width), g_index) for _ in gs]
        + [part_at((width, 2 * ff), 0), part_at((width, ff), d_index)],
        [rows_at(rows, ff), rows_at(rows, 2 * ff)] + [rows_at(rows, width)] * 2 + [halves] * 4,
        [shape_of((n, ff)), shape_of((n, 2 * ff))]
        + [shape_of((n, width))] * 2
        + [shape_of((n // 2, width))] * 4,
        2 * n * width * ff * 6,
        [
            pltpu.VMEM((width, 2 * ff), BF16),
            pltpu.VMEM((width, ff), BF16),
            pltpu.VMEM((rows, width), BF16),
            pltpu.VMEM((rows, width), BF16),
        ],
    )(t, *xs, *gs, w_gu, w_d)


def sum_of(parts):
    total = parts[0][...].astype(F32)
    for p in parts[1:]:
        total = total + p[...].astype(F32)
    return total


def hidden_kernel(n_parts, t, *refs):
    parts = refs[:n_parts]
    x, gains, hidden, normed = refs[n_parts:]
    h = x[...].astype(F32) + sum_of(parts)
    hidden[...] = h
    r = lax.rsqrt(jnp.mean(h * h, axis=1, keepdims=True) + EPS)
    normed[...] = (h * r * gains[1:2, :]).astype(BF16)


def row_tile(rows, width, index=0):
    return pl.BlockSpec((rows // ROW_STEPS, width), lambda i, t: (i, index))


def hidden_call(t, parts, x, gains, rows, width):
    spec = row_tile(rows, width)
    return call(
        functools.partial(hidden_kernel, len(parts)),
        (ROW_STEPS,),
        [spec for _ in parts] + [spec, whole(gains.shape)],
        [spec, spec],
        [shape_of((rows, width), F32), shape_of((rows, width))],
        rows * width * 8,
    )(t, *parts, x, gains)


def norm_back(e, u, gain):
    r = lax.rsqrt(jnp.mean(u * u, axis=1, keepdims=True) + EPS)
    ur = u * r
    ec = e * gain
    return r * (ec - ur * jnp.mean(ur * ec, axis=1, keepdims=True)), jnp.sum(e * ur, axis=0, keepdims=True)


def d_hidden_kernel(n_parts, t, *refs):
    parts = refs[:n_parts]
    hidden, g, gains, d_hidden, branch, d_gain = refs[n_parts:]
    du, dg = norm_back(sum_of(parts), hidden[...], gains[1:2, :])
    d = g[...].astype(F32) + du
    d_hidden[...] = d
    branch[...] = d.astype(BF16)
    accumulate(jnp.broadcast_to(dg, d_gain.shape), d_gain)


def d_hidden_call(t, parts, hidden, g, g_index, gains, rows, width):
    spec = row_tile(rows, width)
    return call(
        functools.partial(d_hidden_kernel, len(parts)),
        (ROW_STEPS,),
        [spec for _ in parts] + [spec, row_tile(rows, width, g_index), whole(gains.shape)],
        [spec, spec, whole((8, width))],
        [shape_of((rows, width), F32), shape_of((rows, width)), shape_of((8, width), F32)],
        rows * width * 12,
    )(t, *parts, hidden, g, gains)


def store_columns(t, reorder, value, out):
    if not reorder:
        out[...] = value
        return
    for p in range(value.shape[1] // HEAD):
        out[:, pl.ds(model_block(t, p), HEAD)] = value[:, p * HEAD : (p + 1) * HEAD]


def activations_kernel(n_parts, reorder, t, *refs):
    parts = refs[:n_parts]
    hidden, out = refs[n_parts:]
    store_columns(t, reorder, (hidden[...] + sum_of(parts)).astype(BF16), out)


def activations_call(t, reorder, parts, hidden, rows, width):
    spec = row_tile(rows, width)
    return call(
        functools.partial(activations_kernel, len(parts), reorder),
        (ROW_STEPS,),
        [spec for _ in parts] + [spec],
        spec,
        shape_of((rows, width)),
        rows * width * 2,
    )(t, *parts, hidden)


def d_tokens_kernel(n_parts, reorder, t, *refs):
    parts = refs[:n_parts]
    x, d_hidden, gains, out = refs[n_parts:]
    du, _ = norm_back(sum_of(parts), x[...].astype(F32), gains[0:1, :])
    store_columns(t, reorder, d_hidden[...] + du, out)


def d_tokens_call(t, reorder, parts, x, d_hidden, gains, rows, width):
    spec = row_tile(rows, width)
    return call(
        functools.partial(d_tokens_kernel, len(parts), reorder),
        (ROW_STEPS,),
        [spec for _ in parts] + [spec, spec, whole(gains.shape)],
        spec,
        shape_of((rows, width), F32),
        rows * width * 12,
    )(t, *parts, x, d_hidden, gains)


def outer_half(left, right, half):
    m = left.shape[1] // 2
    return mm(left[:, half * m : (half + 1) * m], right, 0, 0).astype(BF16)


def shard_of(parts):
    total = parts[0].astype(F32)
    for p in parts[1:]:
        total = total + p.astype(F32)
    return total


def unpack_heads(kv_heads, group, w):
    q, k, v = [], [], []
    for h in range(kv_heads):
        base = h * (group + 2) * HEAD
        mid = base + group * HEAD
        q.append(w[:, base:mid])
        k.append(w[:, mid : mid + HEAD])
        v.append(w[:, mid + HEAD : mid + 2 * HEAD])
    join = lambda parts: jnp.concatenate(parts, axis=1)
    return join(q), join(k), join(v)


def pair_sum_kernel(t, keep, rows, got, *outs):
    n = keep.shape[0] // len(outs)
    for z, out in enumerate(outs):
        here = slice(z * n, (z + 1) * n)
        low = slice(z * GAIN_ROWS, (z + 1) * GAIN_ROWS)
        there = slice(keep.shape[0] + z * GAIN_ROWS, keep.shape[0] + (z + 1) * GAIN_ROWS)
        out[:n, :] = (keep[here, :].astype(F32) + got[here, :].astype(F32)).astype(out.dtype)
        out[n:, :] = (rows[low, :].astype(F32) + got[there, :].astype(F32)).astype(out.dtype)


def pair_sum(t, keep, rows, got, parts):
    m, cols = keep.shape
    n = m // parts + GAIN_ROWS
    return call(
        pair_sum_kernel,
        (1,),
        [whole(keep.shape), whole(rows.shape), whole(got.shape)],
        [whole((n, cols)) for _ in range(parts)],
        [shape_of((n, cols), F32 if z == 0 else BF16) for z in range(parts)],
        m * cols,
    )(t, keep, rows, got)


def xor_pairs(size, bits):
    return [(i, i ^ bits) for i in range(size)]


class Links:
    def __init__(self, dp, tensor):
        self.dp, self.tensor = dp, tensor
        self.direct = (dp, tensor) == (8, 4)
        self.d = lax.axis_index("dp")
        self.t = lax.axis_index("tensor")

    def over_dp(self, x, bits):
        return lax.ppermute(x, "dp", xor_pairs(self.dp, bits))

    def over_tensor(self, x, bits):
        return lax.ppermute(x, "tensor", xor_pairs(self.tensor, bits))

    def offsets(self):
        if self.direct:
            return jnp.stack([self.t, self.d])
        return jnp.zeros((2,), jnp.int32)

    def gather_dp(self, x):
        if not self.direct:
            return [lax.all_gather(x, "dp", axis=0, tiled=True)]
        own = self.gather_z(x)
        return own + [self.over_dp(b, 1) for b in own]

    def gather_z(self, x):
        return [x] + [self.over_dp(x, 2 * z) for z in (1, 2, 3)]

    def send_half(self, left, right):
        send = outer_half(left, right, 1)
        if self.direct:
            send = self.over_dp(send, 1)
        return send, outer_half(left, right, 0)

    def send_quarters(self, got, keep):
        if not self.direct:
            both = jnp.concatenate([keep, got], axis=0)
            return [lax.psum_scatter(both, "dp", scatter_dimension=0, tiled=True)]
        n = keep.shape[0] // 4
        part = lambda z: keep[z * n : (z + 1) * n].astype(F32) + got[z * n : (z + 1) * n].astype(F32)
        return [part(0)] + [self.over_dp(part(z).astype(BF16), 2 * z) for z in (1, 2, 3)]

    def gather_tensor(self, x, *after):
        if not self.direct:
            full = lax.all_gather(x, "tensor", axis=0, tiled=True)
            return jnp.split(full, self.tensor, axis=0)
        far = self.over_tensor(x, 2)
        return [x, self.over_tensor(x, 1), far, self.over_tensor(tie(far, *after) if after else far, 1)]

    def scatter_tensor(self, keep, send, sent=False):
        rows = 2 * keep.shape[0] // self.tensor
        if not self.direct:
            blocks = []
            for k in range(self.tensor // 2):
                blocks += [keep[k * rows : (k + 1) * rows], send[k * rows : (k + 1) * rows]]
            full = jnp.concatenate(blocks, axis=0)
            return [lax.psum_scatter(full, "tensor", scatter_dimension=0, tiled=True)]
        got = send if sent else self.over_tensor(send, 1)
        far = keep[rows:].astype(F32) + got[rows:].astype(F32)
        far = far.astype(BF16)
        return [keep, got, self.over_tensor(far, 2), far]


def rope_tables(offsets):
    frequency = ROPE_BASE ** (-(2.0 * jnp.arange(HEAD // 2, dtype=F32)) / HEAD)
    angles = offsets.astype(F32)[:, None] * frequency[None, :]
    cos, sin = jnp.cos(angles), jnp.sin(angles)
    return jnp.concatenate([cos, cos], axis=1), jnp.concatenate([-sin, sin], axis=1)


def pack_heads(wq, wk, wv, group):
    parts = []
    for h in range(wk.shape[1] // HEAD):
        parts += [
            wq[:, h * group * HEAD : (h + 1) * group * HEAD],
            wk[:, h * HEAD : (h + 1) * HEAD],
            wv[:, h * HEAD : (h + 1) * HEAD],
        ]
    return jnp.concatenate(parts, axis=1)


def body(
    dp,
    tensor,
    tokens,
    segment_ids,
    positions,
    w_query,
    key_projection,
    value_projection,
    w_out,
    w_gate,
    w_up,
    w_down,
    gain_attn,
    gain_mlp,
    gain_query,
    gain_key,
    cotangent,
):
    links = Links(dp, tensor)
    direct = links.direct
    rows, width = tokens.shape
    kv_heads = key_projection.shape[1] // HEAD
    group = w_query.shape[1] // key_projection.shape[1]
    q_cols = group * HEAD
    ff = w_gate.shape[1]
    head_part = HEAD // dp
    t = links.offsets()

    if direct:
        w_attn = pack_attn(
            t,
            w_query,
            key_projection,
            value_projection,
            w_out,
            (gain_attn, gain_mlp, gain_query, gain_key),
            kv_heads,
            group,
        )
        both = pack_rows(t, tie(tokens, w_attn), cotangent)
        w_mlp = pack_mlp(t, tie(w_gate, both), w_up, w_down)
        attn_near = links.gather_z(w_attn)
        attn_far = links.over_dp(w_attn, 1)
        beside = links.over_tensor(both, 1)
        far = links.over_tensor(both, 2)
        across = tie(far, attn_far, attn_near[1], attn_near[2])
        rows_all = [both, beside, far, links.over_tensor(across, 1)]
        w_attn = attn_near + [attn_far] + [links.over_dp(b, 1) for b in attn_near[1:]]
        w_mlp = tie(w_mlp, (far, attn_far, attn_near[1:], w_attn[5]))
        w_qkv, w_o, o_index = w_attn, w_attn, kv_heads * (group + 2) * HEAD // q_cols
        w_gu = w_d = lax.all_gather(w_mlp, "dp", axis=0, tiled=True)
        d_index = 2
        gains = jnp.zeros((8, width), F32)
    else:
        w_qkv = links.gather_dp(pack_heads(w_query, key_projection, value_projection, group))
        w_o = links.gather_dp(w_out.T)
        w_gu = links.gather_dp(jnp.concatenate([w_gate, w_up], axis=1))[0]
        w_d = links.gather_dp(w_down.T)[0]
        d_index, o_index = 0, 0
        row = lambda g: jnp.pad(g, (0, width - g.shape[0]))[None, :].astype(F32)
        whole_gain = lambda g: row(lax.all_gather(g, "dp", axis=0, tiled=True))
        gains = jnp.concatenate(
            [whole_gain(g) for g in (gain_attn, gain_mlp, gain_query, gain_key)]
            + [jnp.zeros((4, width), F32)],
            axis=0,
        )
        rows_all = links.gather_tensor(jnp.concatenate([tokens, cotangent], axis=1))
    own = rows_all[0] if direct else jnp.concatenate([tokens, cotangent], axis=1)

    cos, sin = rope_tables(positions[0])
    seg_row = segment_ids
    seg_col = segment_ids.reshape(-1, 1)

    normed, packed, raw, gains = qkv_call(
        t, rows_all, w_qkv, gains, direct, cos, sin, width, kv_heads, group
    )
    mixed, inv, keep, send = attn_forward(
        t, packed, seg_col, seg_row, w_o, o_index, rows, width, kv_heads, group
    )
    parts = links.scatter_tensor(keep, send)
    hidden, normed_mlp = hidden_call(t, parts[:3], own, gains, rows, width)
    normed_mlp = links.gather_tensor(normed_mlp)
    act, d_gu, normed_mlp, cot, dx_keep, dx_send, out_keep, out_send = mlp_call(
        t, direct, normed_mlp, rows_all, 1, w_gu, w_d, d_index, ff, width
    )
    parts = links.scatter_tensor(dx_keep, dx_send)
    down = links.send_half(cot, tie(act, parts[1:2]))
    d_hidden, branch, d_gain_mlp = d_hidden_call(t, parts[:3], hidden, own, 1, gains, rows, width)
    gu_sum = mm(normed_mlp, tie(d_gu, branch), 0, 0).astype(BF16)
    gu = lax.psum_scatter(gu_sum, "dp", scatter_dimension=0, tiled=True)
    branch = links.gather_tensor(branch, gu_sum, down[0])
    down = links.send_quarters(*down)
    out_parts = links.scatter_tensor(out_keep, tie(out_send, branch))[:3]
    branch_rows = jnp.concatenate(branch, axis=0)
    out_sent = outer_half(branch_rows, mixed, 1)
    if direct:
        out_sent = links.over_dp(out_sent, 1)
    d_packed, d_gain_heads, keep, send, d_gain_attn, *tails = tie(
        attn_backward(
            t, direct, packed, seg_col, seg_row, inv, raw, cos, sin, gains, d_gain_mlp, branch, rows_all,
            w_o, o_index, w_qkv, width, kv_heads, group,
        ),
        out_sent,
        down[1:],
        out_parts,
    )
    if direct:
        send_qkv = jnp.concatenate([outer_half(normed, d_packed, 1), tails[1]], axis=0)
        got = links.over_dp(send_qkv, 1)
    parts = links.scatter_tensor(keep, send)[:3]
    out = (out_sent, outer_half(branch_rows, tie(mixed, parts[:2]), 0))
    out = links.send_quarters(*tie(out, parts[:2]))
    if direct:
        keep_qkv = outer_half(normed, d_packed, 0)
        qkv = pair_sum(t, keep_qkv, tails[0], tie(got, out[1:], parts[2]), 4)
        qkv = [qkv[0]] + [links.over_dp(qkv[z], 2 * z) for z in (1, 2, 3)]
    else:
        qkv = links.send_quarters(*links.send_half(normed, d_packed))
    d_tokens = d_tokens_call(t, direct, parts, own, d_hidden, gains, rows, width)
    activations = activations_call(t, direct, out_parts, hidden, rows, width)
    grad_down = shard_of(down).T
    grad_gate, grad_up = gu[:, :ff].astype(F32), gu[:, ff:].astype(F32)
    grad_out = shard_of(out).T
    n = width // dp
    qkv = shard_of(qkv)
    grad_query, grad_key, grad_value = unpack_heads(kv_heads, group, qkv[:n])
    if direct:
        sums = qkv[n : n + 1, : 4 * HEAD]
        sums = sums + links.over_tensor(sums, 1)
        sums = (sums + links.over_tensor(sums, 2)).reshape(4, HEAD)
        sum_attn, sum_mlp, sum_query, sum_key = sums[0], sums[1], sums[2], sums[3]
    else:
        heads = jnp.sum(d_gain_heads, axis=0)
        sum_attn, sum_mlp, sum_query, sum_key = lax.psum(
            (d_gain_attn[0], d_gain_mlp[0], heads[0], heads[1]), ("dp", "tensor")
        )
        sum_attn = lax.dynamic_slice_in_dim(sum_attn, links.d * n, n, 0)
        sum_mlp = lax.dynamic_slice_in_dim(sum_mlp, links.d * n, n, 0)
    shard = lambda v: lax.dynamic_slice_in_dim(v, links.d * head_part, head_part, 0)
    return (
        activations,
        d_tokens,
        grad_query,
        grad_key,
        grad_value,
        grad_out,
        grad_gate,
        grad_up,
        grad_down,
        sum_attn,
        sum_mlp,
        shard(sum_query),
        shard(sum_key),
    )


def solution(mesh):
    tokens = P(("dp", "tensor"), None)
    by_rows = P("dp", "tensor")
    by_columns = P("tensor", "dp")
    sequence = P("dp", None)
    gain = P("dp")
    return jax.shard_map(
        functools.partial(body, mesh.shape["dp"], mesh.shape["tensor"]),
        mesh=mesh,
        in_specs=(
            tokens,
            sequence,
            sequence,
            by_rows,
            by_rows,
            by_rows,
            by_columns,
            by_rows,
            by_rows,
            by_columns,
            gain,
            gain,
            gain,
            gain,
            tokens,
        ),
        out_specs=(
            tokens,
            tokens,
            by_rows,
            by_rows,
            by_rows,
            by_columns,
            by_rows,
            by_rows,
            by_columns,
            gain,
            gain,
            gain,
            gain,
        ),
        check_vma=False,
    )
```
